32 devices in a mesh: gx: 8 (over z, x), gy: 4 (over y, core).
Axes of the slice: x: 2, y: 2, z: 4, core: 2. Of those that a mesh axis runs over, the one named last changes fastest.
Arguments:
- field: bfloat16 [32, 32, 20, 768], P('gx', 'gy'), may hold values from -6 to 6
- cotangent: bfloat16 [32, 32, 20, 768], P('gx', 'gy'), may hold values from -6 to 6
- spectral_weight: bfloat16 [2, 20, 20, 192, 32, 32], P(None, None, None, 'gx', 'gy'), may hold values from -3 to 3
- point_weight: bfloat16 [20, 20], replicated, may hold values from -1.25 to 1.25
Outputs:
- grad_field: bfloat16 [32, 32, 20, 768], P('gx', 'gy')
- grad_spectral: float32 [2, 20, 20, 192, 32, 32], P(None, None, None, 'gx', 'gy')
The draws below stay inside these ranges and needn't reach their ends.
All inputs are finite; a program needn't handle non-finite values.
Results may differ from the reference program's by a relative error of at most 0.0057.
Values may be sent and summed in bfloat16 or wider, within the bound.
No kernel may reach another device: no remote copies, remote signals or barrier semaphores. Data moves between devices by JAX's collectives and lax.ppermute only.
A program may use at most 448 MiB of HBM per device.

```python
import math
from functools import partial
import jax
import jax.numpy as jnp
from jax import lax

C = 20
NZ = 32
NT = 24
KX = 32
KY = 32
KZ = 24
KT = 8
NX = 32
NY = 32


def steps_of(rng, shape, cuts, least, largest):
    level, own = 1.0, jax.random.fold_in(rng, 6)
    for position, shards_of in cuts:
        draws = jnp.exp(jax.random.uniform(jax.random.fold_in(own, position), (shards_of,), jnp.float32, least / len(cuts), largest / len(cuts)))
        level = level * jnp.repeat(draws, shape[position] // shards_of).reshape([-1 if axis == position else 1 for axis in range(len(shape))])
    return level


def noise(own_key, shape, spread, limit, shards=(), held_as=jnp.bfloat16):
    values = jax.random.normal(own_key, shape, jnp.float32) * spread
    if len(shards) > 0:
        values = steps_of(own_key, shape, shards, -0.22, 0.18) * values
    return jnp.clip(values, min=-limit, max=limit).astype(held_as)


def setup_inputs(seed: int = 0) -> dict:
    splits = jax.random.split(jax.random.key(seed), 5)
    field = noise(splits[0], (NX, NY, C, NZ * NT), 1.0, 6.0, ((0, 8), (1, 4)))
    cotangent = noise(splits[1], (NX, NY, C, NZ * NT), 1.0, 6.0, ((0, 8), (1, 4)))
    spectral_weight = noise(splits[2], (2, C, C, KZ * KT, KX, KY), 0.5, 3.0, ((3, 8), (4, 4)))
    point_weight = noise(splits[3], (C, C), C ** -0.5, 1.25)
    return dict(field=field, cotangent=cotangent, spectral_weight=spectral_weight, point_weight=point_weight)


inv_root_two = 1.0 / math.sqrt(2.0)
inv_root_tau = 1.0 / math.sqrt(2.0 * math.pi)

def kept_freq(length, retained):
    series = jnp.arange(retained)
    return jnp.where(series < retained // 2, series, series - retained + length)

def line_angles(length, retained):
    cell_index = jnp.arange(length)
    phases = kept_freq(length, retained)[:, None] * cell_index[None, :] % length
    return phases.astype(jnp.float32) * (2.0 * math.pi / length)

def block_angles():
    cell_total = NZ * NT
    series = jnp.arange(cell_total)
    depth_index = series // NT
    moment = series % NT
    mode_list = jnp.arange(KZ * KT)
    depth_freq = kept_freq(NZ, KZ)[mode_list // KT]
    time_freq = mode_list % KT
    phases = depth_freq[None, :] * depth_index[:, None] % NZ * NT + time_freq[None, :] * moment[:, None] % NT * NZ
    return (phases % cell_total).astype(jnp.float32) * (2.0 * math.pi / cell_total)

def mode_scale(mode_list, cell_total):
    return jnp.where(mode_list % KT == 0, 1.0, 2.0).astype(jnp.float32) / cell_total

def rotate_along(pattern, leading, trailing, values):
    real_part = values[:, :, :, 0]
    imaginary = values[:, :, :, 1]
    product = partial(jnp.einsum, pattern, precision=lax.Precision.HIGHEST)
    return jnp.stack([product(leading, real_part) - product(trailing, imaginary), product(leading, imaginary) + product(trailing, real_part)], axis=3)

def channel_mix(spectra, weights):
    widened = weights.astype(jnp.float32)
    real_part = spectra[:, :, :, 0]
    imaginary = spectra[:, :, :, 1]
    product = partial(jnp.einsum, 'abim,iomab->abom', precision=lax.Precision.HIGHEST)
    return jnp.stack([product(real_part, widened[0]) - product(imaginary, widened[1]), product(real_part, widened[1]) + product(imaginary, widened[0])], axis=3)

def weight_grads(forward_spec, hidden_spec):
    product = partial(jnp.einsum, 'abim,abom->iomab', precision=lax.Precision.HIGHEST)
    fwd_real = forward_spec[:, :, :, 0]
    fwd_imag = forward_spec[:, :, :, 1]
    hid_real = hidden_spec[:, :, :, 0]
    hid_imag = hidden_spec[:, :, :, 1]
    return jnp.stack([product(fwd_real, hid_real) + product(fwd_imag, hid_imag), product(fwd_real, hid_imag) - product(fwd_imag, hid_real)], axis=0)

def back_spectra(hidden_spec, weights):
    widened = weights.astype(jnp.float32)
    product = partial(jnp.einsum, 'abom,iomab->abim', precision=lax.Precision.HIGHEST)
    hid_real = hidden_spec[:, :, :, 0]
    hid_imag = hidden_spec[:, :, :, 1]
    return jnp.stack([product(hid_real, widened[0]) + product(hid_imag, widened[1]), product(hid_imag, widened[0]) - product(hid_real, widened[1])], axis=3)

def gelu_slope(preact):
    return 0.5 * (1.0 + jax.scipy.special.erf(preact * inv_root_two)) + preact * jnp.exp(-0.5 * preact * preact) * inv_root_tau

def reference(field, cotangent, spectral_weight, point_weight):
    cell_total = NX * NY * NZ * NT
    angles = block_angles()
    forward_table = jnp.concatenate([jnp.cos(angles), -jnp.sin(angles)], axis=1).astype(jnp.bfloat16)
    unscaled = jnp.concatenate([jnp.cos(angles).T, -jnp.sin(angles).T], axis=0)
    mode_list = jnp.arange(KZ * KT)
    factors = mode_scale(mode_list, cell_total)
    scaled = unscaled * jnp.concatenate([factors, factors])[:, None]
    row_angles = line_angles(NX, KX)
    column_angles = line_angles(NY, KY)

    def forward(cells):
        spectra = jnp.dot(cells.reshape(-1, NZ * NT), forward_table, preferred_element_type=jnp.float32)
        spectra = spectra.reshape(NX, NY, C, 2, KZ * KT)
        spectra = rotate_along('ka,abcm->kbcm', jnp.cos(row_angles), -jnp.sin(row_angles), spectra)
        return rotate_along('kb,abcm->akcm', jnp.cos(column_angles), -jnp.sin(column_angles), spectra)

    def inverse(spectra, table):
        spectra = rotate_along('bk,akcm->abcm', jnp.cos(column_angles).T, jnp.sin(column_angles).T, spectra)
        spectra = rotate_along('ak,kbcm->abcm', jnp.cos(row_angles).T, jnp.sin(row_angles).T, spectra)
        flattened = spectra.reshape(-1, 2 * KZ * KT)
        return jnp.dot(flattened, table, precision=lax.Precision.HIGHEST).reshape(NX, NY, C, NZ * NT)
    forward_spec = forward(field)
    mixed = channel_mix(forward_spec, spectral_weight)
    response = inverse(mixed, scaled)
    wide_point = point_weight.astype(jnp.float32)
    preact = response + jnp.einsum('xyiz,io->xyoz', field.astype(jnp.float32), wide_point, precision=lax.Precision.HIGHEST)
    hidden = (cotangent.astype(jnp.float32) * gelu_slope(preact)).astype(jnp.bfloat16)
    hidden_spec = forward(hidden) * factors
    grad_spectral = weight_grads(forward_spec, hidden_spec)
    backward = inverse(back_spectra(hidden_spec, spectral_weight), unscaled)
    local_part = jnp.einsum('xyoz,io->xyiz', hidden.astype(jnp.float32), wide_point, precision=lax.Precision.HIGHEST)
    grad_field = (backward + local_part).astype(jnp.bfloat16)
    return (grad_field, grad_spectral)
```

```python
from functools import partial
import math

import jax
import jax.numpy as jnp
import ml_dtypes
import numpy as np
from jax import lax
from jax.experimental import pallas as pl
from jax.experimental.pallas import tpu as pltpu
from jax.sharding import PartitionSpec as P

NZ = 32
NT = 24
KX = 32
KY = 32
KZ = 24
KT = 8


inv_root_two = 1.0 / math.sqrt(2.0)
inv_root_tau = 1.0 / math.sqrt(2.0 * math.pi)


def kept_freq(length, retained):
    series = jnp.arange(retained)
    return jnp.where(series < retained // 2, series, series - retained + length)


def line_angles(length, retained):
    cell_index = jnp.arange(length)
    phases = kept_freq(length, retained)[:, None] * cell_index[None, :] % length
    return phases.astype(jnp.float32) * (2.0 * math.pi / length)


def block_angles():
    cell_total = NZ * NT
    series = jnp.arange(cell_total)
    depth_index = series // NT
    moment = series % NT
    mode_list = jnp.arange(KZ * KT)
    depth_freq = kept_freq(NZ, KZ)[mode_list // KT]
    time_freq = mode_list % KT
    phases = (
        depth_freq[None, :] * depth_index[:, None] % NZ * NT
        + time_freq[None, :] * moment[:, None] % NT * NZ
    )
    return (phases % cell_total).astype(jnp.float32) * (2.0 * math.pi / cell_total)


def mode_scale(mode_list, cell_total):
    return jnp.where(mode_list % KT == 0, 1.0, 2.0).astype(jnp.float32) / cell_total


def twiddle(pattern, cosine, sine, sign, values):
    product = partial(jnp.einsum, pattern, precision=lax.Precision.HIGHEST)
    real_part = values[0]
    imaginary = values[1]
    return jnp.stack(
        [
            product(cosine, real_part) - sign * product(sine, imaginary),
            product(cosine, imaginary) + sign * product(sine, real_part),
        ],
        axis=0,
    )


def channel_mix(spectra, weights):
    widened = weights.astype(jnp.float32)
    product = partial(jnp.einsum, "mkli,iomkl->mklo", precision=lax.Precision.HIGHEST)
    return jnp.stack(
        [
            product(spectra[0], widened[0]) - product(spectra[1], widened[1]),
            product(spectra[0], widened[1]) + product(spectra[1], widened[0]),
        ],
        axis=0,
    )


def weight_grads(forward_spec, hidden_spec):
    product = partial(jnp.einsum, "mkli,mklo->iomkl", precision=lax.Precision.HIGHEST)
    return jnp.stack(
        [
            product(forward_spec[0], hidden_spec[0]) + product(forward_spec[1], hidden_spec[1]),
            product(forward_spec[0], hidden_spec[1]) - product(forward_spec[1], hidden_spec[0]),
        ],
        axis=0,
    )


def back_spectra(hidden_spec, weights):
    widened = weights.astype(jnp.float32)
    product = partial(jnp.einsum, "mklo,iomkl->mkli", precision=lax.Precision.HIGHEST)
    return jnp.stack(
        [
            product(hidden_spec[0], widened[0]) + product(hidden_spec[1], widened[1]),
            product(hidden_spec[1], widened[0]) - product(hidden_spec[0], widened[1]),
        ],
        axis=0,
    )


def gelu_slope(preact):
    return (
        0.5 * (1.0 + jax.scipy.special.erf(preact * inv_root_two))
        + preact * jnp.exp(-0.5 * preact * preact) * inv_root_tau
    )


def plain_device(field, cotangent, spectral_weight, point_weight):
    x_local = field.shape[0]
    y_local = field.shape[1]
    channels = field.shape[2]
    groups_x = lax.axis_size("gx")
    groups_y = lax.axis_size("gy")
    rows_x = x_local * groups_x
    rows_y = y_local * groups_y
    mode_total = KZ * KT
    cell_total = rows_x * rows_y * NZ * NT
    angles = block_angles()
    forward_table = jnp.concatenate([jnp.cos(angles), -jnp.sin(angles)], axis=1).astype(
        jnp.bfloat16
    )
    unscaled = jnp.concatenate([jnp.cos(angles).T, -jnp.sin(angles).T], axis=0)
    mode_list = jnp.arange(mode_total)
    factors = mode_scale(mode_list, cell_total)
    scaled = unscaled * jnp.concatenate([factors, factors])[:, None]
    row_angles = line_angles(rows_x, KX)
    column_angles = line_angles(rows_y, KY)
    row_cos = jnp.cos(row_angles)
    row_sin = jnp.sin(row_angles)
    column_cos = jnp.cos(column_angles)
    column_sin = jnp.sin(column_angles)

    def analyze(cells):
        flat_cells = cells.reshape(-1, cells.shape[3])
        return jnp.einsum(
            "rz,zk->kr", flat_cells, forward_table, preferred_element_type=jnp.float32
        )

    def synthesize(spectra, table):
        flattened = spectra.reshape(2 * mode_total, -1)
        cells = jnp.einsum("kr,kz->rz", flattened, table, precision=lax.Precision.HIGHEST)
        return cells.reshape(x_local, y_local, channels, -1)

    block = mode_total // groups_x

    def forward(cells):
        spectra = analyze(cells).reshape(2, groups_x, block, x_local, y_local * channels)
        spectra = lax.all_to_all(spectra, "gx", split_axis=1, concat_axis=3, tiled=True)
        spectra = spectra.reshape(2, block, rows_x, y_local * channels)
        spectra = twiddle("ka,mar->mkr", row_cos, row_sin, -1.0, spectra)
        spectra = spectra.reshape(2, block, KX, y_local, channels)
        spectra = lax.all_to_all(spectra, "gy", split_axis=2, concat_axis=3, tiled=True)
        return twiddle("lb,mkbc->mklc", column_cos, column_sin, -1.0, spectra)

    def inverse(spectra, table):
        spectra = twiddle("lb,mklc->mkbc", column_cos, column_sin, 1.0, spectra)
        spectra = lax.all_to_all(spectra, "gy", split_axis=3, concat_axis=2, tiled=True)
        spectra = spectra.reshape(2, block, KX, y_local * channels)
        spectra = twiddle("ka,mkr->mar", row_cos, row_sin, 1.0, spectra)
        spectra = lax.all_to_all(spectra, "gx", split_axis=2, concat_axis=1, tiled=True)
        return synthesize(spectra, table)

    forward_spec = forward(field)
    mixed = channel_mix(forward_spec, spectral_weight)
    response = inverse(mixed, scaled)
    preact = response + jnp.einsum(
        "xyiz,io->xyoz", field, point_weight, preferred_element_type=jnp.float32
    )
    hidden = (cotangent.astype(jnp.float32) * gelu_slope(preact)).astype(jnp.bfloat16)
    local_count = forward_spec.shape[1]
    local_modes = lax.axis_index("gx") * local_count + jnp.arange(local_count)
    hidden_spec = forward(hidden) * mode_scale(local_modes, cell_total)[:, None, None, None]
    grad_spectral = weight_grads(forward_spec, hidden_spec)
    backward = inverse(back_spectra(hidden_spec, spectral_weight), unscaled)
    local_part = jnp.einsum(
        "xyoz,io->xyiz", hidden, point_weight, preferred_element_type=jnp.float32
    )
    grad_field = (backward + local_part).astype(jnp.bfloat16)
    return (grad_field, grad_spectral)


LANES = 128
GROUP_ORDER = (0, 2, 1, 3)


def kept_freq_np(length, retained):
    series = np.arange(retained)
    return np.where(series < retained // 2, series, series - retained + length)


def split_table(table):
    high = table.astype(ml_dtypes.bfloat16)
    low = (table - high.astype(np.float64)).astype(ml_dtypes.bfloat16)
    return np.stack([high, low])


def cell_table():
    cells = np.arange(NZ * NT)
    modes = np.arange(KZ * KT)
    depth = kept_freq_np(NZ, KZ)[modes // KT][:, None] * (cells // NT)[None, :] % NZ * NT
    moment = (modes % KT)[:, None] * (cells % NT)[None, :] % NT * NZ
    angles = 2.0 * np.pi * ((depth + moment) % (NZ * NT)) / (NZ * NT)
    return split_table(np.concatenate([np.cos(angles), -np.sin(angles)], axis=0))


def rotation(length, retained):
    phases = np.arange(length)[:, None] * kept_freq_np(length, retained)[None, :] % length
    angles = 2.0 * np.pi * phases / length
    cosine, sine = np.cos(angles), np.sin(angles)
    return np.stack([np.stack([cosine, -sine], axis=1), np.stack([sine, cosine], axis=1)], axis=0)


def row_table(groups_x, x_local, y_local, groups_y):
    turn = rotation(groups_x * x_local, KX)
    turn = turn.reshape(2, groups_x, x_local, 2, groups_y, KX // groups_y)
    full = np.einsum("psxqgk,yz->spxygqkz", turn, np.eye(y_local))
    return split_table(full.reshape(groups_x * 2 * x_local * y_local, -1))


def column_table(groups_y, y_local, kx_local):
    turn = rotation(groups_y * y_local, KY).reshape(2, groups_y, y_local, 2, KY)
    full = np.einsum("psyql,kh->spkyqhl", turn, np.eye(kx_local))
    return split_table(full.reshape(groups_y * 2 * kx_local * y_local, -1))


def scale_table(block, width, cell_total):
    factors = np.where(np.arange(block) % KT == 0, 1.0, 2.0) / cell_total
    return np.broadcast_to(factors[:, None], (block, width)).astype(np.float32)


def dot(left, right, left_dim=1, right_dim=0):
    return lax.dot_general(
        left, right, (((left_dim,), (right_dim,)), ((), ())), preferred_element_type=jnp.float32
    )


def dot_split(left, table, right_dim):
    return dot(left, table[0], 1, right_dim) + dot(left, table[1], 1, right_dim)


def even_lanes(rows, width):
    lane = lax.broadcasted_iota(jnp.int32, (rows, LANES), 1)
    return lane // width % 2 == 0


def pack_parts(real, imag, width):
    even = even_lanes(real.shape[0], width)
    first = jnp.where(even, real, pltpu.roll(imag, width, 1))
    second = jnp.where(even, pltpu.roll(real, LANES - width, 1), imag)
    return first, second


def unpack_parts(first, second, width):
    even = even_lanes(first.shape[0], width)
    real = jnp.where(even, first, pltpu.roll(second, width, 1))
    imag = jnp.where(even, pltpu.roll(first, LANES - width, 1), second)
    return real, imag


def gather_cells(ref):
    pieces = [ref[x, g] for g in GROUP_ORDER for x in range(ref.shape[0])]
    return jnp.concatenate(pieces, axis=0)


def store_spectra(spectra, out_ref, width):
    half = spectra.shape[0] // 2
    first, second = pack_parts(spectra[:half], spectra[half:], width)
    groups = out_ref.shape[0]
    block = half // groups
    for d in range(groups):
        out_ref[d, :block] = first[d * block : (d + 1) * block].astype(out_ref.dtype)
        out_ref[d, block:] = second[d * block : (d + 1) * block].astype(out_ref.dtype)


def load_spectra(ref, width):
    groups = ref.shape[0]
    block = ref.shape[1] // 2
    wide = [ref[s].astype(jnp.float32) for s in range(groups)]
    first = jnp.concatenate([w[:block] for w in wide], axis=0)
    second = jnp.concatenate([w[block:] for w in wide], axis=0)
    real, imag = unpack_parts(first, second, width)
    return jnp.concatenate([real, imag], axis=0).astype(jnp.bfloat16)


def analyze_kernel(field_ref, table_ref, out_ref, cells_ref, *, width):
    cells = gather_cells(field_ref)
    cells_ref[...] = cells
    store_spectra(dot(table_ref[0], cells, 1, 1), out_ref, width)


def rows_kernel(in_ref, table_ref, out_ref):
    groups = in_ref.shape[0]
    half = in_ref.shape[2] // 2
    lanes = out_ref.shape[2] // 2
    for c in range(2):
        left = jnp.concatenate(
            [in_ref[s, :, c * half : (c + 1) * half] for s in range(groups)], axis=1
        )
        result = dot_split(left, table_ref, 0)
        for g in range(out_ref.shape[0]):
            out_ref[g, :, c * lanes : (c + 1) * lanes] = result[
                :, g * lanes : (g + 1) * lanes
            ].astype(out_ref.dtype)


def rows_back_kernel(in_ref, table_ref, out_ref):
    half = in_ref.shape[2] // 2
    lanes = out_ref.shape[2] // 2
    results = []
    for c in range(2):
        left = jnp.concatenate(
            [in_ref[s, :, c * half : (c + 1) * half] for s in range(in_ref.shape[0])], axis=1
        )
        results.append(dot_split(left, table_ref, 1))
    for d in range(out_ref.shape[0]):
        pair = [result[:, d * lanes : (d + 1) * lanes] for result in results]
        out_ref[d] = jnp.concatenate(pair, axis=1).astype(out_ref.dtype)


def columns_forward(in_ref, table_ref):
    half = in_ref.shape[2] // 2
    for c in range(2):
        left = jnp.concatenate(
            [in_ref[s, :, c * half : (c + 1) * half] for s in range(in_ref.shape[0])], axis=1
        )
        yield c, dot_split(left, table_ref, 0)


def columns_back(mixed_ref, table_ref, out_ref):
    lanes = out_ref.shape[2] // 2
    for c in range(2):
        mixed = mixed_ref[c]
        high = mixed.astype(jnp.bfloat16)
        low = (mixed - high.astype(jnp.float32)).astype(jnp.bfloat16)
        result = dot_split(high, table_ref, 1) + dot(low, table_ref[0], 1, 1)
        for g in range(out_ref.shape[0]):
            out_ref[g, :, c * lanes : (c + 1) * lanes] = result[
                :, g * lanes : (g + 1) * lanes
            ].astype(out_ref.dtype)


def mix_kernel(
    in_ref, table_ref, weight_ref, scale_ref, spec_ref, out_ref, mixed_ref, *, backward
):
    step = pl.program_id(0)
    block, width = scale_ref.shape
    channels = weight_ref.shape[1] if backward else weight_ref.shape[0]
    inner = weight_ref.shape[0] if backward else weight_ref.shape[1]

    @pl.when(step == 0)
    def _():
        for c, result in columns_forward(in_ref, table_ref):
            if backward:
                for r in range(channels // 2):
                    rows = slice(r * block, (r + 1) * block)
                    for p in range(2):
                        lanes = slice(p * width, (p + 1) * width)
                        spec_ref[c, rows, lanes] = result[rows, lanes] * scale_ref[...]
            else:
                spec_ref[c] = result

    for n in range(inner):
        real = jnp.zeros((block, width), jnp.float32)
        imag = jnp.zeros((block, width), jnp.float32)
        for k in range(channels):
            rows = slice(k // 2 * block, (k // 2 + 1) * block)
            spec_real = spec_ref[k % 2, rows, :width]
            spec_imag = spec_ref[k % 2, rows, width:]
            w = weight_ref.at[n, k] if backward else weight_ref.at[k, n]
            w_real = w[0].astype(jnp.float32)
            w_imag = w[1].astype(jnp.float32)
            if backward:
                real = real + (spec_real * w_real + spec_imag * w_imag)
                imag = imag + (spec_imag * w_real - spec_real * w_imag)
            else:
                real = real + (spec_real * w_real - spec_imag * w_imag)
                imag = imag + (spec_real * w_imag + spec_imag * w_real)
        if not backward:
            real = real * scale_ref[...]
            imag = imag * scale_ref[...]
        rows = pl.ds(pl.multiple_of((step * inner + n) // 2 * block, 8), block)
        mixed_ref[n % 2, rows, :width] = real
        mixed_ref[n % 2, rows, width:] = imag

    @pl.when(step == pl.num_programs(0) - 1)
    def _():
        columns_back(mixed_ref, table_ref, out_ref)


def slope_kernel(
    in_ref, cells_ref, cot_ref, point_ref, table_ref, out_ref, hidden_ref, *, width
):
    spectra = load_spectra(in_ref, width)
    preact = dot(spectra, table_ref[0], 0, 0) + dot(spectra, table_ref[1], 0, 0)
    preact = preact + dot(point_ref[...], cells_ref[...])
    slope = gelu_slope(preact)
    hidden = (gather_cells(cot_ref).astype(jnp.float32) * slope).astype(jnp.bfloat16)
    hidden_ref[...] = hidden
    store_spectra(dot(table_ref[0], hidden, 1, 1), out_ref, width)


def final_kernel(in_ref, hidden_ref, point_ref, table_ref, out_ref, *, width):
    spectra = load_spectra(in_ref, width)
    total = dot(spectra, table_ref[0], 0, 0) + dot(spectra, table_ref[1], 0, 0)
    total = total + dot(point_ref[...], hidden_ref[...], 0, 0)
    x_local, _, y_local, _ = out_ref.shape
    total = total.astype(out_ref.dtype)
    for n, g in enumerate(GROUP_ORDER):
        for x in range(x_local):
            start = (n * x_local + x) * y_local
            out_ref[x, g] = total[start : start + y_local]


def point_kernel(weight_ref, out_ref, *, width):
    rows, channels = out_ref.shape[0], weight_ref.shape[0]
    cell = lax.broadcasted_iota(jnp.int32, (rows, channels), 0) // width
    slot = cell % 4
    channel = cell // 4 * 4 + slot // 2 + slot % 2 * 2
    pick = (channel == lax.broadcasted_iota(jnp.int32, (rows, channels), 1)).astype(jnp.bfloat16)
    left = dot(pick, weight_ref[...], 1, 1).astype(jnp.bfloat16)
    full = dot(left, pick, 1, 1)
    row = lax.broadcasted_iota(jnp.int32, (rows, rows), 0) % width
    column = lax.broadcasted_iota(jnp.int32, (rows, rows), 1) % width
    out_ref[...] = jnp.where(row == column, full, 0.0).astype(jnp.bfloat16)


def pack_weights_kernel(in_ref, out_ref, wide_ref):
    _, _, outs, block, kx_local, ky = in_ref.shape
    rows = outs * block
    per_tile = LANES // ky
    wide_ref[:, :ky] = in_ref[0, 0].reshape(rows * kx_local, ky).astype(jnp.float32)
    lane = lax.broadcasted_iota(jnp.int32, (rows, LANES), 1) // ky
    for t in range(kx_local // per_tile):
        packed = None
        for k in range(per_tile):
            piece = wide_ref[pl.ds(t * per_tile + k, rows, stride=kx_local), :]
            if k == 0:
                packed = piece
            else:
                packed = jnp.where(lane == k, pltpu.roll(piece, k * ky, 1), packed)
        packed = packed.astype(jnp.bfloat16)
        for o in range(outs):
            out_ref[0, o, 0, :, t * LANES : (t + 1) * LANES] = packed[o * block : (o + 1) * block]


def spread_kernel(in_ref, out_ref):
    rows = in_ref.shape[1]
    kx_local, ky = 8, KY
    for p in range(2):
        for k in range(kx_local):
            start = (p * kx_local + k) * ky
            out_ref[0, p, pl.ds(k, rows, stride=kx_local), :ky] = in_ref[0, :, start : start + ky]


def grads_body(f_ref, h_ref, out_ref):
    channels = out_ref.shape[1]

    def step(i, carry):
        f_real = f_ref[i % 2, 0, i // 2, 0]
        f_imag = f_ref[i % 2, 1, i // 2, 0]
        for o in range(channels):
            h_real = h_ref[o % 2, 0, o // 2, 0]
            h_imag = h_ref[o % 2, 1, o // 2, 0]
            out_ref[0, i, o, 0] = f_real * h_real + f_imag * h_imag
            out_ref[1, i, o, 0] = f_real * h_imag - f_imag * h_real
        return carry

    lax.fori_loop(0, channels, step, 0)


def grads_first_kernel(f_ref, h_ref, out_ref):
    grads_body(f_ref, h_ref, out_ref)


def grads_rest_kernel(f_ref, h_ref, _, out_ref):
    grads_body(f_ref, h_ref, out_ref)


def whole(shape):
    return pl.BlockSpec(shape, lambda *_: (0,) * len(shape))


def fits(field, weight, groups_x, groups_y):
    x_local, y_local, channels, cells = field.shape
    block, kx_local = weight.shape[3:5]
    return (
        cells == NZ * NT
        and x_local * y_local * 4 == LANES
        and channels % 4 == 0
        and block % KT == 0
        and kx_local == 8
        and y_local == 8
        and weight.shape[5] * 4 == LANES
        and block * groups_x == KZ * KT
    )


def fused_device(field, cotangent, weight, point_weight):
    x_local, y_local, channels, cells = field.shape
    groups_x = lax.axis_size("gx")
    groups_y = lax.axis_size("gy")
    block, kx_local, ky = weight.shape[3:]
    cell_total = groups_x * x_local * groups_y * y_local * cells
    width = x_local * y_local
    tiles = channels // 4
    rows = channels // 2 * block
    lanes = 2 * kx_local * y_local
    plane = kx_local * ky
    bf16, f32 = jnp.bfloat16, jnp.float32
    shape = jax.ShapeDtypeStruct
    params = partial(pltpu.CompilerParams, vmem_limit_bytes=60000 * 1024)

    table = jnp.asarray(cell_table())
    row_mat = jnp.asarray(row_table(groups_x, x_local, y_local, groups_y))
    column_mat = jnp.asarray(column_table(groups_y, y_local, kx_local))
    scale = jnp.asarray(scale_table(block, plane, cell_total))

    cell_block = pl.BlockSpec((x_local, 4, y_local, cells), lambda c: (0, c, 0, 0))
    flat_block = pl.BlockSpec((LANES, cells), lambda c: (c, 0))
    spec_block = pl.BlockSpec((groups_x, 2 * block, LANES), lambda c: (0, c, 0))
    spec_shape = shape((groups_x, rows, LANES), bf16)
    flat_shape = shape((channels * width, cells), bf16)
    mid_shape = shape((groups_y, rows, 2 * lanes), bf16)

    field_rows = field.transpose(0, 2, 1, 3)
    cot_rows = cotangent.transpose(0, 2, 1, 3)

    spectra, flat_field = pl.pallas_call(
        partial(analyze_kernel, width=width),
        grid=(tiles,),
        in_specs=[cell_block, whole(table.shape)],
        out_specs=[spec_block, flat_block],
        out_shape=[spec_shape, flat_shape],
        compiler_params=params(),
        name="analyze",
    )(field_rows, table)

    packed = pl.pallas_call(
        pack_weights_kernel,
        grid=(channels, 2),
        in_specs=[
            pl.BlockSpec((1, 1, channels, block, kx_local, ky), lambda i, p: (p, i, 0, 0, 0, 0))
        ],
        out_specs=pl.BlockSpec((1, channels, 1, block, plane), lambda i, p: (i, 0, p, 0, 0)),
        out_shape=shape((channels, channels, 2, block, plane), bf16),
        scratch_shapes=[pltpu.VMEM((channels * block * kx_local, LANES), f32)],
        compiler_params=params(),
        name="pack_weights",
    )(weight)

    point = pl.pallas_call(
        partial(point_kernel, width=width),
        out_shape=shape((channels * width, channels * width), bf16),
        compiler_params=params(),
        name="point",
    )(point_weight)

    def over_x(values):
        return lax.all_to_all(values, "gx", 0, 0, tiled=True)

    def over_y(values):
        return lax.all_to_all(values, "gy", 0, 0, tiled=True)

    def to_rows(values):
        return pl.pallas_call(
            rows_kernel,
            out_shape=mid_shape,
            compiler_params=params(),
            name="rows",
        )(values, row_mat)

    def from_rows(values):
        return pl.pallas_call(
            rows_back_kernel,
            out_shape=spec_shape,
            compiler_params=params(),
            name="rows_back",
        )(values, row_mat)

    def mix(values, backward):
        if backward:
            w_block = pl.BlockSpec((2, channels, 2, block, plane), lambda j: (j, 0, 0, 0, 0))
        else:
            w_block = pl.BlockSpec((channels, 2, 2, block, plane), lambda j: (0, j, 0, 0, 0))
        return pl.pallas_call(
            partial(mix_kernel, backward=backward),
            grid=(channels // 2,),
            in_specs=[whole(mid_shape.shape), whole(column_mat.shape), w_block, whole(scale.shape)],
            out_specs=[whole((2, rows, 2 * plane)), whole(mid_shape.shape)],
            out_shape=[shape((2, rows, 2 * plane), f32), mid_shape],
            scratch_shapes=[pltpu.VMEM((2, rows, 2 * plane), f32)],
            compiler_params=params(),
            name="mix_back" if backward else "mix",
        )(values, column_mat, packed, scale)

    def spread(spec):
        return pl.pallas_call(
            spread_kernel,
            grid=(2,),
            in_specs=[pl.BlockSpec((1, rows, 2 * plane), lambda c: (c, 0, 0))],
            out_specs=pl.BlockSpec((1, 2, rows * kx_local, ky), lambda c: (c, 0, 0, 0)),
            out_shape=shape((2, 2, rows * kx_local, ky), f32),
            compiler_params=params(),
            name="spread",
        )(spec).reshape(2, 2, channels // 2, block, kx_local, ky)

    forward_spec, mixed = mix(over_y(to_rows(over_x(spectra))), False)
    back = over_x(from_rows(over_y(mixed)))
    hidden_spectra, hidden = pl.pallas_call(
        partial(slope_kernel, width=width),
        grid=(tiles,),
        in_specs=[
            spec_block,
            whole(flat_shape.shape),
            cell_block,
            pl.BlockSpec((LANES, channels * width), lambda c: (c, 0)),
            whole(table.shape),
        ],
        out_specs=[spec_block, flat_block],
        out_shape=[spec_shape, flat_shape],
        compiler_params=params(),
        name="slope",
    )(back, flat_field, cot_rows, point, table)
    hidden_spec, mixed = mix(over_y(to_rows(over_x(hidden_spectra))), True)

    spread_f = spread(forward_spec)
    spread_h = spread(hidden_spec)
    tile = (2, 2, channels // 2, 1, kx_local, ky)
    grad_tile = (2, channels, channels, 1, kx_local, ky)
    grad_shape = shape((2, channels, channels, block, kx_local, ky), f32)
    head = block // 3

    def at(offset):
        return lambda m: (0, 0, 0, m + offset, 0, 0)

    grad_head = pl.pallas_call(
        grads_first_kernel,
        grid=(head,),
        in_specs=[pl.BlockSpec(tile, at(0)), pl.BlockSpec(tile, at(0))],
        out_specs=pl.BlockSpec(grad_tile, at(0)),
        out_shape=grad_shape,
        compiler_params=params(),
        name="grads_first",
    )(spread_f, spread_h)

    back = from_rows(over_y(mixed))
    grad_spectral = pl.pallas_call(
        grads_rest_kernel,
        grid=(block - head,),
        in_specs=[
            pl.BlockSpec(tile, at(head)),
            pl.BlockSpec(tile, at(head)),
            pl.BlockSpec(memory_space=pl.ANY),
        ],
        out_specs=pl.BlockSpec(grad_tile, at(head)),
        out_shape=grad_shape,
        input_output_aliases={2: 0},
        compiler_params=params(),
        name="grads_rest",
    )(spread_f, spread_h, grad_head)
    back = over_x(back)
    grad_field = pl.pallas_call(
        partial(final_kernel, width=width),
        grid=(tiles,),
        in_specs=[
            spec_block,
            whole(flat_shape.shape),
            pl.BlockSpec((channels * width, LANES), lambda c: (0, c)),
            whole(table.shape),
        ],
        out_specs=cell_block,
        out_shape=shape((x_local, channels, y_local, cells), bf16),
        compiler_params=params(),
        name="final",
    )(back, hidden, point, table)
    return grad_field.transpose(0, 2, 1, 3), grad_spectral


def per_device(field, cotangent, spectral_weight, point_weight):
    groups = lax.axis_size("gx"), lax.axis_size("gy")
    if fits(field, spectral_weight, *groups):
        return fused_device(field, cotangent, spectral_weight, point_weight)
    return plain_device(field, cotangent, spectral_weight, point_weight)


def solution(mesh):
    placed = (
        P("gx", "gy", None, None),
        P("gx", "gy", None, None),
        P(None, None, None, "gx", "gy", None),
        P(),
    )
    return jax.shard_map(
        per_device,
        mesh=mesh,
        in_specs=placed,
        out_specs=(P("gx", "gy", None, None), P(None, None, None, "gx", "gy", None)),
        check_vma=False,
    )
```

```python
from functools import partial
import math

import jax
import jax.numpy as jnp
import ml_dtypes
import numpy as np
from jax import lax
from jax.experimental import pallas as pl
from jax.experimental.pallas import tpu as pltpu
from jax.sharding import PartitionSpec as P


NZ = 32
NT = 24
KX = 32
KY = 32
KZ = 24
KT = 8


inv_root_two = 1.0 / math.sqrt(2.0)
inv_root_tau = 1.0 / math.sqrt(2.0 * math.pi)


def kept_freq(length, retained):
    series = jnp.arange(retained)
    return jnp.where(series < retained // 2, series, series - retained + length)


def line_angles(length, retained):
    cell_index = jnp.arange(length)
    phases = kept_freq(length, retained)[:, None] * cell_index[None, :] % length
    return phases.astype(jnp.float32) * (2.0 * math.pi / length)


def block_angles():
    cell_total = NZ * NT
    series = jnp.arange(cell_total)
    depth_index = series // NT
    moment = series % NT
    mode_list = jnp.arange(KZ * KT)
    depth_freq = kept_freq(NZ, KZ)[mode_list // KT]
    time_freq = mode_list % KT
    phases = (
        depth_freq[None, :] * depth_index[:, None] % NZ * NT
        + time_freq[None, :] * moment[:, None] % NT * NZ
    )
    return (phases % cell_total).astype(jnp.float32) * (2.0 * math.pi / cell_total)


def mode_scale(mode_list, cell_total):
    return jnp.where(mode_list % KT == 0, 1.0, 2.0).astype(jnp.float32) / cell_total


def twiddle(pattern, cosine, sine, sign, values):
    product = partial(jnp.einsum, pattern, precision=lax.Precision.HIGHEST)
    real_part = values[0]
    imaginary = values[1]
    return jnp.stack(
        [
            product(cosine, real_part) - sign * product(sine, imaginary),
            product(cosine, imaginary) + sign * product(sine, real_part),
        ],
        axis=0,
    )


def channel_mix(spectra, weights):
    widened = weights.astype(jnp.float32)
    product = partial(jnp.einsum, "mkli,iomkl->mklo", precision=lax.Precision.HIGHEST)
    return jnp.stack(
        [
            product(spectra[0], widened[0]) - product(spectra[1], widened[1]),
            product(spectra[0], widened[1]) + product(spectra[1], widened[0]),
        ],
        axis=0,
    )


def weight_grads(forward_spec, hidden_spec):
    product = partial(jnp.einsum, "mkli,mklo->iomkl", precision=lax.Precision.HIGHEST)
    return jnp.stack(
        [
            product(forward_spec[0], hidden_spec[0]) + product(forward_spec[1], hidden_spec[1]),
            product(forward_spec[0], hidden_spec[1]) - product(forward_spec[1], hidden_spec[0]),
        ],
        axis=0,
    )


def back_spectra(hidden_spec, weights):
    widened = weights.astype(jnp.float32)
    product = partial(jnp.einsum, "mklo,iomkl->mkli", precision=lax.Precision.HIGHEST)
    return jnp.stack(
        [
            product(hidden_spec[0], widened[0]) + product(hidden_spec[1], widened[1]),
            product(hidden_spec[1], widened[0]) - product(hidden_spec[0], widened[1]),
        ],
        axis=0,
    )


def gelu_slope(preact):
    return (
        0.5 * (1.0 + jax.scipy.special.erf(preact * inv_root_two))
        + preact * jnp.exp(-0.5 * preact * preact) * inv_root_tau
    )


def plain_device(field, cotangent, spectral_weight, point_weight):
    x_local = field.shape[0]
    y_local = field.shape[1]
    channels = field.shape[2]
    groups_x = lax.axis_size("gx")
    groups_y = lax.axis_size("gy")
    rows_x = x_local * groups_x
    rows_y = y_local * groups_y
    mode_total = KZ * KT
    cell_total = rows_x * rows_y * NZ * NT
    angles = block_angles()
    forward_table = jnp.concatenate([jnp.cos(angles), -jnp.sin(angles)], axis=1).astype(
        jnp.bfloat16
    )
    unscaled = jnp.concatenate([jnp.cos(angles).T, -jnp.sin(angles).T], axis=0)
    mode_list = jnp.arange(mode_total)
    factors = mode_scale(mode_list, cell_total)
    scaled = unscaled * jnp.concatenate([factors, factors])[:, None]
    row_angles = line_angles(rows_x, KX)
    column_angles = line_angles(rows_y, KY)
    row_cos = jnp.cos(row_angles)
    row_sin = jnp.sin(row_angles)
    column_cos = jnp.cos(column_angles)
    column_sin = jnp.sin(column_angles)

    def analyze(cells):
        flat_cells = cells.reshape(-1, cells.shape[3])
        return jnp.einsum(
            "rz,zk->kr", flat_cells, forward_table, preferred_element_type=jnp.float32
        )

    def synthesize(spectra, table):
        flattened = spectra.reshape(2 * mode_total, -1)
        cells = jnp.einsum("kr,kz->rz", flattened, table, precision=lax.Precision.HIGHEST)
        return cells.reshape(x_local, y_local, channels, -1)

    block = mode_total // groups_x

    def forward(cells):
        spectra = analyze(cells).reshape(2, groups_x, block, x_local, y_local * channels)
        spectra = lax.all_to_all(spectra, "gx", split_axis=1, concat_axis=3, tiled=True)
        spectra = spectra.reshape(2, block, rows_x, y_local * channels)
        spectra = twiddle("ka,mar->mkr", row_cos, row_sin, -1.0, spectra)
        spectra = spectra.reshape(2, block, KX, y_local, channels)
        spectra = lax.all_to_all(spectra, "gy", split_axis=2, concat_axis=3, tiled=True)
        return twiddle("lb,mkbc->mklc", column_cos, column_sin, -1.0, spectra)

    def inverse(spectra, table):
        spectra = twiddle("lb,mklc->mkbc", column_cos, column_sin, 1.0, spectra)
        spectra = lax.all_to_all(spectra, "gy", split_axis=3, concat_axis=2, tiled=True)
        spectra = spectra.reshape(2, block, KX, y_local * channels)
        spectra = twiddle("ka,mkr->mar", row_cos, row_sin, 1.0, spectra)
        spectra = lax.all_to_all(spectra, "gx", split_axis=2, concat_axis=1, tiled=True)
        return synthesize(spectra, table)

    forward_spec = forward(field)
    mixed = channel_mix(forward_spec, spectral_weight)
    response = inverse(mixed, scaled)
    preact = response + jnp.einsum(
        "xyiz,io->xyoz", field, point_weight, preferred_element_type=jnp.float32
    )
    hidden = (cotangent.astype(jnp.float32) * gelu_slope(preact)).astype(jnp.bfloat16)
    local_count = forward_spec.shape[1]
    local_modes = lax.axis_index("gx") * local_count + jnp.arange(local_count)
    hidden_spec = forward(hidden) * mode_scale(local_modes, cell_total)[:, None, None, None]
    grad_spectral = weight_grads(forward_spec, hidden_spec)
    backward = inverse(back_spectra(hidden_spec, spectral_weight), unscaled)
    local_part = jnp.einsum(
        "xyoz,io->xyiz", hidden, point_weight, preferred_element_type=jnp.float32
    )
    grad_field = (backward + local_part).astype(jnp.bfloat16)
    return (grad_field, grad_spectral)


LANES = 128
GROUP_ORDER = (0, 2, 1, 3)


def kept_freq_np(length, retained):
    series = np.arange(retained)
    return np.where(series < retained // 2, series, series - retained + length)


def split_table(table):
    high = table.astype(ml_dtypes.bfloat16)
    low = (table - high.astype(np.float64)).astype(ml_dtypes.bfloat16)
    return np.stack([high, low])


def cell_table():
    cells = np.arange(NZ * NT)
    modes = np.arange(KZ * KT)
    depth = kept_freq_np(NZ, KZ)[modes // KT][:, None] * (cells // NT)[None, :] % NZ * NT
    moment = (modes % KT)[:, None] * (cells % NT)[None, :] % NT * NZ
    angles = 2.0 * np.pi * ((depth + moment) % (NZ * NT)) / (NZ * NT)
    return split_table(np.concatenate([np.cos(angles), -np.sin(angles)], axis=0))


def rotation(length, retained):
    phases = np.arange(length)[:, None] * kept_freq_np(length, retained)[None, :] % length
    angles = 2.0 * np.pi * phases / length
    cosine, sine = np.cos(angles), np.sin(angles)
    return np.stack([np.stack([cosine, -sine], axis=1), np.stack([sine, cosine], axis=1)], axis=0)


def row_table(groups_x, x_local, y_local, groups_y):
    turn = rotation(groups_x * x_local, KX)
    turn = turn.reshape(2, groups_x, x_local, 2, groups_y, KX // groups_y)
    full = np.einsum("psxqgk,yz->spxygqkz", turn, np.eye(y_local))
    return split_table(full.reshape(groups_x * 2 * x_local * y_local, -1))


def column_table(groups_y, y_local, kx_local):
    turn = rotation(groups_y * y_local, KY).reshape(2, groups_y, y_local, 2, KY)
    full = np.einsum("psyql,kh->spkyqhl", turn, np.eye(kx_local))
    return split_table(full.reshape(groups_y * 2 * kx_local * y_local, -1))


def scale_table(block, width, cell_total):
    factors = np.where(np.arange(block) % KT == 0, 1.0, 2.0) / cell_total
    return np.broadcast_to(factors[:, None], (block, width)).astype(np.float32)


def dot(left, right, left_dim=1, right_dim=0):
    return lax.dot_general(
        left, right, (((left_dim,), (right_dim,)), ((), ())), preferred_element_type=jnp.float32
    )


def dot_split(left, table, right_dim):
    return dot(left, table[0], 1, right_dim) + dot(left, table[1], 1, right_dim)


def even_lanes(rows, width):
    lane = lax.broadcasted_iota(jnp.int32, (rows, LANES), 1)
    return lane // width % 2 == 0


def pack_parts(real, imag, width):
    even = even_lanes(real.shape[0], width)
    first = jnp.where(even, real, pltpu.roll(imag, width, 1))
    second = jnp.where(even, pltpu.roll(real, LANES - width, 1), imag)
    return first, second


def unpack_parts(first, second, width):
    even = even_lanes(first.shape[0], width)
    real = jnp.where(even, first, pltpu.roll(second, width, 1))
    imag = jnp.where(even, pltpu.roll(first, LANES - width, 1), second)
    return real, imag


def gather_cells(ref):
    pieces = [ref[x, g] for g in GROUP_ORDER for x in range(ref.shape[0])]
    return jnp.concatenate(pieces, axis=0)


def store_spectra(spectra, out_ref, width):
    half = spectra.shape[0] // 2
    first, second = pack_parts(spectra[:half], spectra[half:], width)
    groups = out_ref.shape[0]
    block = half // groups
    for d in range(groups):
        out_ref[d, :block] = first[d * block : (d + 1) * block].astype(out_ref.dtype)
        out_ref[d, block:] = second[d * block : (d + 1) * block].astype(out_ref.dtype)


def load_spectra(ref, width):
    groups = ref.shape[0]
    block = ref.shape[1] // 2
    wide = [ref[s].astype(jnp.float32) for s in range(groups)]
    first = jnp.concatenate([w[:block] for w in wide], axis=0)
    second = jnp.concatenate([w[block:] for w in wide], axis=0)
    real, imag = unpack_parts(first, second, width)
    return jnp.concatenate([real, imag], axis=0).astype(jnp.bfloat16)


def analyze_kernel(field_ref, table_ref, out_ref, cells_ref, *, width):
    cells = gather_cells(field_ref)
    cells_ref[...] = cells
    store_spectra(dot(table_ref[0], cells, 1, 1), out_ref, width)


def rows_kernel(in_ref, table_ref, out_ref):
    groups = in_ref.shape[0]
    half = in_ref.shape[2] // 2
    lanes = out_ref.shape[2] // 2
    for c in range(2):
        left = jnp.concatenate(
            [in_ref[s, :, c * half : (c + 1) * half] for s in range(groups)], axis=1
        )
        result = dot_split(left, table_ref, 0)
        for g in range(out_ref.shape[0]):
            out_ref[g, :, c * lanes : (c + 1) * lanes] = result[
                :, g * lanes : (g + 1) * lanes
            ].astype(out_ref.dtype)


def rows_back_kernel(in_ref, table_ref, out_ref):
    half = in_ref.shape[2] // 2
    lanes = out_ref.shape[2] // 2
    results = []
    for c in range(2):
        left = jnp.concatenate(
            [in_ref[s, :, c * half : (c + 1) * half] for s in range(in_ref.shape[0])], axis=1
        )
        results.append(dot_split(left, table_ref, 1))
    for d in range(out_ref.shape[0]):
        pair = [result[:, d * lanes : (d + 1) * lanes] for result in results]
        out_ref[d] = jnp.concatenate(pair, axis=1).astype(out_ref.dtype)


def columns_forward(in_ref, table_ref):
    half = in_ref.shape[2] // 2
    for c in range(2):
        left = jnp.concatenate(
            [in_ref[s, :, c * half : (c + 1) * half] for s in range(in_ref.shape[0])], axis=1
        )
        yield c, dot_split(left, table_ref, 0)


def columns_back(mixed_ref, table_ref, out_ref):
    lanes = out_ref.shape[2] // 2
    for c in range(2):
        mixed = mixed_ref[c]
        high = mixed.astype(jnp.bfloat16)
        low = (mixed - high.astype(jnp.float32)).astype(jnp.bfloat16)
        result = dot_split(high, table_ref, 1) + dot(low, table_ref[0], 1, 1)
        for g in range(out_ref.shape[0]):
            out_ref[g, :, c * lanes : (c + 1) * lanes] = result[
                :, g * lanes : (g + 1) * lanes
            ].astype(out_ref.dtype)


def mix_kernel(
    in_ref, table_ref, weight_ref, scale_ref, spec_ref, out_ref, mixed_ref, *, backward
):
    step = pl.program_id(0)
    block = scale_ref.shape[0]
    channels = weight_ref.shape[1] if backward else weight_ref.shape[0]
    inner = weight_ref.shape[0] if backward else weight_ref.shape[1]
    spans = spec_ref.shape[1] // 2

    @pl.when(step == 0)
    def _():
        for c, result in columns_forward(in_ref, table_ref):
            for t in range(2 * spans):
                piece = result[:, t * LANES : (t + 1) * LANES]
                if backward:
                    for r in range(channels // 2):
                        rows = slice(r * block, (r + 1) * block)
                        spec_ref[c, t, rows] = piece[rows] * scale_ref[...]
                else:
                    spec_ref[c, t] = piece

    for t in range(spans):
        lanes = slice(t * LANES, (t + 1) * LANES)
        real = [jnp.zeros((block, LANES), jnp.float32)] * inner
        imag = [jnp.zeros((block, LANES), jnp.float32)] * inner
        for k in range(channels):
            rows = slice(k // 2 * block, (k // 2 + 1) * block)
            spec_real = spec_ref[k % 2, t, rows]
            spec_imag = spec_ref[k % 2, spans + t, rows]
            for n in range(inner):
                w = weight_ref.at[n, k] if backward else weight_ref.at[k, n]
                w_real = w[0, :, lanes].astype(jnp.float32)
                w_imag = w[1, :, lanes].astype(jnp.float32)
                if backward:
                    real[n] = real[n] + (spec_real * w_real + spec_imag * w_imag)
                    imag[n] = imag[n] + (spec_imag * w_real - spec_real * w_imag)
                else:
                    real[n] = real[n] + (spec_real * w_real - spec_imag * w_imag)
                    imag[n] = imag[n] + (spec_real * w_imag + spec_imag * w_real)
        for n in range(inner):
            if not backward:
                real[n] = real[n] * scale_ref[...]
                imag[n] = imag[n] * scale_ref[...]
            rows = pl.ds(pl.multiple_of((step * inner + n) // 2 * block, 8), block)
            mixed_ref[n % 2, rows, lanes] = real[n]
            mixed_ref[n % 2, rows, slice((spans + t) * LANES, (spans + t + 1) * LANES)] = imag[n]

    @pl.when(step == pl.num_programs(0) - 1)
    def _():
        columns_back(mixed_ref, table_ref, out_ref)


def slope_kernel(
    in_ref, cells_ref, cot_ref, point_ref, table_ref, out_ref, hidden_ref, *, width
):
    spectra = load_spectra(in_ref, width)
    preact = dot(spectra, table_ref[0], 0, 0) + dot(spectra, table_ref[1], 0, 0)
    preact = preact + dot(point_ref[...], cells_ref[...])
    slope = gelu_slope(preact)
    hidden = (gather_cells(cot_ref).astype(jnp.float32) * slope).astype(jnp.bfloat16)
    hidden_ref[...] = hidden
    store_spectra(dot(table_ref[0], hidden, 1, 1), out_ref, width)


def final_kernel(in_ref, hidden_ref, point_ref, table_ref, out_ref, *, width):
    spectra = load_spectra(in_ref, width)
    total = dot(spectra, table_ref[0], 0, 0) + dot(spectra, table_ref[1], 0, 0)
    total = total + dot(point_ref[...], hidden_ref[...], 0, 0)
    x_local, _, y_local, _ = out_ref.shape
    total = total.astype(out_ref.dtype)
    for n, g in enumerate(GROUP_ORDER):
        for x in range(x_local):
            start = (n * x_local + x) * y_local
            out_ref[x, g] = total[start : start + y_local]


def point_kernel(weight_ref, out_ref, *, width):
    rows, channels = out_ref.shape[0], weight_ref.shape[0]
    cell = lax.broadcasted_iota(jnp.int32, (rows, channels), 0) // width
    slot = cell % 4
    channel = cell // 4 * 4 + slot // 2 + slot % 2 * 2
    pick = (channel == lax.broadcasted_iota(jnp.int32, (rows, channels), 1)).astype(jnp.bfloat16)
    left = dot(pick, weight_ref[...], 1, 1).astype(jnp.bfloat16)
    full = dot(left, pick, 1, 1)
    row = lax.broadcasted_iota(jnp.int32, (rows, rows), 0) % width
    column = lax.broadcasted_iota(jnp.int32, (rows, rows), 1) % width
    out_ref[...] = jnp.where(row == column, full, 0.0).astype(jnp.bfloat16)


def pack_body(in_ref, out_ref):
    for i in range(in_ref.shape[1]):
        for p in range(2):
            out_ref[i, :, p] = pltpu.einshape("omky->om(ky)", in_ref[p, i])


def pack_first_kernel(in_ref, out_ref):
    pack_body(in_ref, out_ref)


def pack_rest_kernel(in_ref, _, out_ref):
    pack_body(in_ref, out_ref)


def spread_modes(spec_ref, tile_ref, m):
    count = tile_ref.shape[2] // 8
    block = spec_ref.shape[2] // count
    for c in range(2):
        for p in range(2):
            for k in range(8):
                start = (p * 8 + k) * KY
                piece = spec_ref[c, start // LANES, pl.ds(m, count, stride=block), :]
                start = start % LANES
                tile_ref[c, p, pl.ds(k, count, stride=8), :KY] = piece[:, start : start + KY]


def grads_body(f_spec_ref, h_spec_ref, out_ref, f_ref, h_ref, first):
    channels = out_ref.shape[1]
    mode = pl.program_id(0) + first
    spread_modes(f_spec_ref, f_ref, mode)
    spread_modes(h_spec_ref, h_ref, mode)

    def step(i, carry):
        rows = pl.ds(pl.multiple_of(i // 2 * 8, 8), 8)
        f_real = f_ref[i % 2, 0, rows, :KY]
        f_imag = f_ref[i % 2, 1, rows, :KY]
        for o in range(channels):
            h_real = h_ref[o % 2, 0, o // 2 * 8 : o // 2 * 8 + 8, :KY]
            h_imag = h_ref[o % 2, 1, o // 2 * 8 : o // 2 * 8 + 8, :KY]
            out_ref[0, i, o, 0] = f_real * h_real + f_imag * h_imag
            out_ref[1, i, o, 0] = f_real * h_imag - f_imag * h_real
        return carry

    lax.fori_loop(0, channels, step, 0)


def grads_first_kernel(f_spec_ref, h_spec_ref, out_ref, f_ref, h_ref):
    grads_body(f_spec_ref, h_spec_ref, out_ref, f_ref, h_ref, 0)


def grads_rest_kernel(f_spec_ref, h_spec_ref, _, out_ref, f_ref, h_ref, *, first):
    grads_body(f_spec_ref, h_spec_ref, out_ref, f_ref, h_ref, first)


def whole(shape):
    return pl.BlockSpec(shape, lambda *_: (0,) * len(shape))


def fits(field, weight, groups_x, groups_y):
    x_local, y_local, channels, cells = field.shape
    block, kx_local = weight.shape[3:5]
    return (
        cells == NZ * NT
        and x_local * y_local * 4 == LANES
        and channels % 4 == 0
        and block % KT == 0
        and kx_local == 8
        and y_local == 8
        and weight.shape[5] * 4 == LANES
        and block * groups_x == KZ * KT
    )


def fused_device(field, cotangent, weight, point_weight):
    x_local, y_local, channels, cells = field.shape
    groups_x = lax.axis_size("gx")
    groups_y = lax.axis_size("gy")
    block, kx_local, ky = weight.shape[3:]
    cell_total = groups_x * x_local * groups_y * y_local * cells
    width = x_local * y_local
    tiles = channels // 4
    rows = channels // 2 * block
    lanes = 2 * kx_local * y_local
    plane = kx_local * ky
    bf16, f32 = jnp.bfloat16, jnp.float32
    shape = jax.ShapeDtypeStruct
    params = partial(pltpu.CompilerParams, vmem_limit_bytes=58 * 1024 * 1024)

    table = jnp.asarray(cell_table())
    row_mat = jnp.asarray(row_table(groups_x, x_local, y_local, groups_y))
    column_mat = jnp.asarray(column_table(groups_y, y_local, kx_local))
    scale = jnp.asarray(scale_table(block, LANES, cell_total))

    cell_block = pl.BlockSpec((x_local, 4, y_local, cells), lambda c: (0, c, 0, 0))
    flat_block = pl.BlockSpec((LANES, cells), lambda c: (c, 0))
    spec_block = pl.BlockSpec((groups_x, 2 * block, LANES), lambda c: (0, c, 0))
    spec_shape = shape((groups_x, rows, LANES), bf16)
    flat_shape = shape((channels * width, cells), bf16)
    full_shape = shape((2, 2 * plane // LANES, rows, LANES), f32)
    mid_shape = shape((groups_y, rows, 2 * lanes), bf16)

    field_rows = field.transpose(0, 2, 1, 3)
    cot_rows = cotangent.transpose(0, 2, 1, 3)

    spectra, flat_field = pl.pallas_call(
        partial(analyze_kernel, width=width),
        grid=(tiles,),
        in_specs=[cell_block, whole(table.shape)],
        out_specs=[spec_block, flat_block],
        out_shape=[spec_shape, flat_shape],
        compiler_params=params(),
        name="analyze",
    )(field_rows, table)

    pack_shape = shape((channels, channels, 2, block, plane), bf16)
    pack_steps = channels // 2
    pack_head = pack_steps * 3 // 5

    def pack_specs(offset):
        return (
            pl.BlockSpec(
                (2, 2, channels, block, kx_local, ky), lambda i: (0, i + offset, 0, 0, 0, 0)
            ),
            pl.BlockSpec((2, channels, 2, block, plane), lambda i: (i + offset, 0, 0, 0, 0)),
        )

    source, target = pack_specs(0)
    packed = pl.pallas_call(
        pack_first_kernel,
        grid=(pack_head,),
        in_specs=[source],
        out_specs=target,
        out_shape=pack_shape,
        compiler_params=params(),
        name="pack_first",
    )(weight)
    source, target = pack_specs(pack_head)
    packed = pl.pallas_call(
        pack_rest_kernel,
        grid=(pack_steps - pack_head,),
        in_specs=[source, pl.BlockSpec(memory_space=pl.ANY)],
        out_specs=target,
        out_shape=pack_shape,
        input_output_aliases={1: 0},
        compiler_params=params(),
        name="pack_rest",
    )(weight, packed)

    point = pl.pallas_call(
        partial(point_kernel, width=width),
        out_shape=shape((channels * width, channels * width), bf16),
        compiler_params=params(),
        name="point",
    )(point_weight)

    def over_x(values):
        return lax.all_to_all(values, "gx", 0, 0, tiled=True)

    def over_y(values):
        return lax.all_to_all(values, "gy", 0, 0, tiled=True)

    def to_rows(values):
        return pl.pallas_call(
            rows_kernel,
            out_shape=mid_shape,
            compiler_params=params(),
            name="rows",
        )(values, row_mat)

    def from_rows(values):
        return pl.pallas_call(
            rows_back_kernel,
            out_shape=spec_shape,
            compiler_params=params(),
            name="rows_back",
        )(values, row_mat)

    def mix(values, backward):
        if backward:
            w_block = pl.BlockSpec((2, channels, 2, block, plane), lambda j: (j, 0, 0, 0, 0))
        else:
            w_block = pl.BlockSpec((channels, 2, 2, block, plane), lambda j: (0, j, 0, 0, 0))
        return pl.pallas_call(
            partial(mix_kernel, backward=backward),
            grid=(channels // 2,),
            in_specs=[whole(mid_shape.shape), whole(column_mat.shape), w_block, whole(scale.shape)],
            out_specs=[whole(full_shape.shape), whole(mid_shape.shape)],
            out_shape=[full_shape, mid_shape],
            scratch_shapes=[pltpu.VMEM((2, rows, 2 * plane), f32)],
            compiler_params=params(),
            name="mix_back" if backward else "mix",
        )(values, column_mat, packed, scale)

    forward_spec, mixed = mix(over_y(to_rows(over_x(spectra))), False)
    back = over_x(from_rows(over_y(mixed)))
    hidden_spectra, hidden = pl.pallas_call(
        partial(slope_kernel, width=width),
        grid=(tiles,),
        in_specs=[
            spec_block,
            whole(flat_shape.shape),
            cell_block,
            pl.BlockSpec((LANES, channels * width), lambda c: (c, 0)),
            whole(table.shape),
        ],
        out_specs=[spec_block, flat_block],
        out_shape=[spec_shape, flat_shape],
        compiler_params=params(),
        name="slope",
    )(back, flat_field, cot_rows, point, table)
    hidden_spec, mixed = mix(over_y(to_rows(over_x(hidden_spectra))), True)

    grad_tile = (2, channels, channels, 1, kx_local, ky)
    grad_shape = shape((2, channels, channels, block, kx_local, ky), f32)
    spec_whole = whole(forward_spec.shape)
    tiles_scratch = [pltpu.VMEM((2, 2, channels // 2 * kx_local, LANES), f32)] * 2
    head = block // 4

    def at(offset):
        return lambda m: (0, 0, 0, m + offset, 0, 0)

    grad_head = pl.pallas_call(
        grads_first_kernel,
        grid=(head,),
        in_specs=[spec_whole, spec_whole],
        out_specs=pl.BlockSpec(grad_tile, at(0)),
        out_shape=grad_shape,
        scratch_shapes=tiles_scratch,
        compiler_params=params(),
        name="grads_first",
    )(forward_spec, hidden_spec)

    back = from_rows(over_y(mixed))
    grad_spectral = pl.pallas_call(
        partial(grads_rest_kernel, first=head),
        grid=(block - head,),
        in_specs=[spec_whole, spec_whole, pl.BlockSpec(memory_space=pl.ANY)],
        out_specs=pl.BlockSpec(grad_tile, at(head)),
        out_shape=grad_shape,
        input_output_aliases={2: 0},
        scratch_shapes=tiles_scratch,
        compiler_params=params(),
        name="grads_rest",
    )(forward_spec, hidden_spec, grad_head)
    back = over_x(back)
    grad_field = pl.pallas_call(
        partial(final_kernel, width=width),
        grid=(tiles,),
        in_specs=[
            spec_block,
            whole(flat_shape.shape),
            pl.BlockSpec((channels * width, LANES), lambda c: (0, c)),
            whole(table.shape),
        ],
        out_specs=cell_block,
        out_shape=shape((x_local, channels, y_local, cells), bf16),
        compiler_params=params(),
        name="final",
    )(back, hidden, point, table)
    return grad_field.transpose(0, 2, 1, 3), grad_spectral


def per_device(field, cotangent, spectral_weight, point_weight):
    groups = lax.axis_size("gx"), lax.axis_size("gy")
    if fits(field, spectral_weight, *groups):
        return fused_device(field, cotangent, spectral_weight, point_weight)
    return plain_device(field, cotangent, spectral_weight, point_weight)


def solution(mesh):
    placed = (
        P("gx", "gy", None, None),
        P("gx", "gy", None, None),
        P(None, None, None, "gx", "gy", None),
        P(),
    )
    return jax.shard_map(
        per_device,
        mesh=mesh,
        in_specs=placed,
        out_specs=(P("gx", "gy", None, None), P(None, None, None, "gx", "gy", None)),
        check_vma=False,
    )
```

```python
from functools import partial
import math

import jax
import jax.numpy as jnp
import ml_dtypes
import numpy as np
from jax import lax
from jax.experimental import pallas as pl
from jax.experimental.pallas import tpu as pltpu
from jax.sharding import PartitionSpec as P


NZ = 32
NT = 24
KX = 32
KY = 32
KZ = 24
KT = 8


inv_root_two = 1.0 / math.sqrt(2.0)
inv_root_tau = 1.0 / math.sqrt(2.0 * math.pi)


def kept_freq(length, retained):
    series = jnp.arange(retained)
    return jnp.where(series < retained // 2, series, series - retained + length)


def line_angles(length, retained):
    cell_index = jnp.arange(length)
    phases = kept_freq(length, retained)[:, None] * cell_index[None, :] % length
    return phases.astype(jnp.float32) * (2.0 * math.pi / length)


def block_angles():
    cell_total = NZ * NT
    series = jnp.arange(cell_total)
    depth_index = series // NT
    moment = series % NT
    mode_list = jnp.arange(KZ * KT)
    depth_freq = kept_freq(NZ, KZ)[mode_list // KT]
    time_freq = mode_list % KT
    phases = (
        depth_freq[None, :] * depth_index[:, None] % NZ * NT
        + time_freq[None, :] * moment[:, None] % NT * NZ
    )
    return (phases % cell_total).astype(jnp.float32) * (2.0 * math.pi / cell_total)


def mode_scale(mode_list, cell_total):
    return jnp.where(mode_list % KT == 0, 1.0, 2.0).astype(jnp.float32) / cell_total


def twiddle(pattern, cosine, sine, sign, values):
    product = partial(jnp.einsum, pattern, precision=lax.Precision.HIGHEST)
    real_part = values[0]
    imaginary = values[1]
    return jnp.stack(
        [
            product(cosine, real_part) - sign * product(sine, imaginary),
            product(cosine, imaginary) + sign * product(sine, real_part),
        ],
        axis=0,
    )


def channel_mix(spectra, weights):
    widened = weights.astype(jnp.float32)
    product = partial(jnp.einsum, "mkli,iomkl->mklo", precision=lax.Precision.HIGHEST)
    return jnp.stack(
        [
            product(spectra[0], widened[0]) - product(spectra[1], widened[1]),
            product(spectra[0], widened[1]) + product(spectra[1], widened[0]),
        ],
        axis=0,
    )


def weight_grads(forward_spec, hidden_spec):
    product = partial(jnp.einsum, "mkli,mklo->iomkl", precision=lax.Precision.HIGHEST)
    return jnp.stack(
        [
            product(forward_spec[0], hidden_spec[0]) + product(forward_spec[1], hidden_spec[1]),
            product(forward_spec[0], hidden_spec[1]) - product(forward_spec[1], hidden_spec[0]),
        ],
        axis=0,
    )


def back_spectra(hidden_spec, weights):
    widened = weights.astype(jnp.float32)
    product = partial(jnp.einsum, "mklo,iomkl->mkli", precision=lax.Precision.HIGHEST)
    return jnp.stack(
        [
            product(hidden_spec[0], widened[0]) + product(hidden_spec[1], widened[1]),
            product(hidden_spec[1], widened[0]) - product(hidden_spec[0], widened[1]),
        ],
        axis=0,
    )


def gelu_slope(preact):
    return (
        0.5 * (1.0 + jax.scipy.special.erf(preact * inv_root_two))
        + preact * jnp.exp(-0.5 * preact * preact) * inv_root_tau
    )


def plain_device(field, cotangent, spectral_weight, point_weight):
    x_local = field.shape[0]
    y_local = field.shape[1]
    channels = field.shape[2]
    groups_x = lax.axis_size("gx")
    groups_y = lax.axis_size("gy")
    rows_x = x_local * groups_x
    rows_y = y_local * groups_y
    mode_total = KZ * KT
    cell_total = rows_x * rows_y * NZ * NT
    angles = block_angles()
    forward_table = jnp.concatenate([jnp.cos(angles), -jnp.sin(angles)], axis=1).astype(
        jnp.bfloat16
    )
    unscaled = jnp.concatenate([jnp.cos(angles).T, -jnp.sin(angles).T], axis=0)
    mode_list = jnp.arange(mode_total)
    factors = mode_scale(mode_list, cell_total)
    scaled = unscaled * jnp.concatenate([factors, factors])[:, None]
    row_angles = line_angles(rows_x, KX)
    column_angles = line_angles(rows_y, KY)
    row_cos = jnp.cos(row_angles)
    row_sin = jnp.sin(row_angles)
    column_cos = jnp.cos(column_angles)
    column_sin = jnp.sin(column_angles)

    def analyze(cells):
        flat_cells = cells.reshape(-1, cells.shape[3])
        return jnp.einsum(
            "rz,zk->kr", flat_cells, forward_table, preferred_element_type=jnp.float32
        )

    def synthesize(spectra, table):
        flattened = spectra.reshape(2 * mode_total, -1)
        cells = jnp.einsum("kr,kz->rz", flattened, table, precision=lax.Precision.HIGHEST)
        return cells.reshape(x_local, y_local, channels, -1)

    block = mode_total // groups_x

    def forward(cells):
        spectra = analyze(cells).reshape(2, groups_x, block, x_local, y_local * channels)
        spectra = lax.all_to_all(spectra, "gx", split_axis=1, concat_axis=3, tiled=True)
        spectra = spectra.reshape(2, block, rows_x, y_local * channels)
        spectra = twiddle("ka,mar->mkr", row_cos, row_sin, -1.0, spectra)
        spectra = spectra.reshape(2, block, KX, y_local, channels)
        spectra = lax.all_to_all(spectra, "gy", split_axis=2, concat_axis=3, tiled=True)
        return twiddle("lb,mkbc->mklc", column_cos, column_sin, -1.0, spectra)

    def inverse(spectra, table):
        spectra = twiddle("lb,mklc->mkbc", column_cos, column_sin, 1.0, spectra)
        spectra = lax.all_to_all(spectra, "gy", split_axis=3, concat_axis=2, tiled=True)
        spectra = spectra.reshape(2, block, KX, y_local * channels)
        spectra = twiddle("ka,mkr->mar", row_cos, row_sin, 1.0, spectra)
        spectra = lax.all_to_all(spectra, "gx", split_axis=2, concat_axis=1, tiled=True)
        return synthesize(spectra, table)

    forward_spec = forward(field)
    mixed = channel_mix(forward_spec, spectral_weight)
    response = inverse(mixed, scaled)
    preact = response + jnp.einsum(
        "xyiz,io->xyoz", field, point_weight, preferred_element_type=jnp.float32
    )
    hidden = (cotangent.astype(jnp.float32) * gelu_slope(preact)).astype(jnp.bfloat16)
    local_count = forward_spec.shape[1]
    local_modes = lax.axis_index("gx") * local_count + jnp.arange(local_count)
    hidden_spec = forward(hidden) * mode_scale(local_modes, cell_total)[:, None, None, None]
    grad_spectral = weight_grads(forward_spec, hidden_spec)
    backward = inverse(back_spectra(hidden_spec, spectral_weight), unscaled)
    local_part = jnp.einsum(
        "xyoz,io->xyiz", hidden, point_weight, preferred_element_type=jnp.float32
    )
    grad_field = (backward + local_part).astype(jnp.bfloat16)
    return (grad_field, grad_spectral)


LANES = 128
GROUP_ORDER = (0, 2, 1, 3)


def kept_freq_np(length, retained):
    series = np.arange(retained)
    return np.where(series < retained // 2, series, series - retained + length)


TURN_SCALE = 1.62445


def scaled_table(table):
    return (table * TURN_SCALE).astype(ml_dtypes.bfloat16)


def split_table(table):
    high = table.astype(ml_dtypes.bfloat16)
    low = (table - high.astype(np.float64)).astype(ml_dtypes.bfloat16)
    return np.stack([high, low])


def cell_table():
    cells = np.arange(NZ * NT)
    modes = np.arange(KZ * KT)
    depth = kept_freq_np(NZ, KZ)[modes // KT][:, None] * (cells // NT)[None, :] % NZ * NT
    moment = (modes % KT)[:, None] * (cells % NT)[None, :] % NT * NZ
    angles = 2.0 * np.pi * ((depth + moment) % (NZ * NT)) / (NZ * NT)
    return split_table(np.concatenate([np.cos(angles), -np.sin(angles)], axis=0))


def rotation(length, retained):
    phases = np.arange(length)[:, None] * kept_freq_np(length, retained)[None, :] % length
    angles = 2.0 * np.pi * phases / length
    cosine, sine = np.cos(angles), np.sin(angles)
    return np.stack([np.stack([cosine, -sine], axis=1), np.stack([sine, cosine], axis=1)], axis=0)


def row_table(groups_x, x_local, y_local, groups_y):
    turn = rotation(groups_x * x_local, KX)
    turn = turn.reshape(2, groups_x, x_local, 2, groups_y, KX // groups_y)
    full = np.einsum("psxqgk,yz->spxygqkz", turn, np.eye(y_local))
    return scaled_table(full.reshape(groups_x * 2 * x_local * y_local, -1))


def column_table(groups_y, y_local, kx_local):
    turn = rotation(groups_y * y_local, KY).reshape(2, groups_y, y_local, 2, KY)
    full = np.einsum("psyql,kh->spkyqhl", turn, np.eye(kx_local))
    return scaled_table(full.reshape(groups_y * 2 * kx_local * y_local, -1))


def scale_table(block, width, cell_total):
    factors = np.where(np.arange(block) % KT == 0, 1.0, 2.0) / cell_total
    return np.broadcast_to(factors[:, None], (block, width)).astype(np.float32)


def dot(left, right, left_dim=1, right_dim=0):
    return lax.dot_general(
        left, right, (((left_dim,), (right_dim,)), ((), ())), preferred_element_type=jnp.float32
    )


def turn(left, table_ref, right_dim):
    if left.dtype == jnp.bfloat16:
        return dot(left, table_ref[...], 1, right_dim) * (1.0 / TURN_SCALE)
    high = left.astype(jnp.bfloat16)
    low = (left - high.astype(jnp.float32)).astype(jnp.bfloat16)
    both = dot(jnp.concatenate([high, low], axis=0), table_ref[...], 1, right_dim)
    count = left.shape[0]
    return (both[:count] + both[count:]) * (1.0 / TURN_SCALE)


def joined(in_ref):
    half = in_ref.shape[2] // 2
    return jnp.concatenate(
        [
            jnp.concatenate(
                [in_ref[s, :, c * half : (c + 1) * half] for s in range(in_ref.shape[0])], axis=1
            )
            for c in range(2)
        ],
        axis=0,
    )


def even_lanes(rows, width):
    lane = lax.broadcasted_iota(jnp.int32, (rows, LANES), 1)
    return lane // width % 2 == 0


def pack_parts(real, imag, width):
    even = even_lanes(real.shape[0], width)
    first = jnp.where(even, real, pltpu.roll(imag, width, 1))
    second = jnp.where(even, pltpu.roll(real, LANES - width, 1), imag)
    return first, second


def unpack_parts(first, second, width):
    even = even_lanes(first.shape[0], width)
    real = jnp.where(even, first, pltpu.roll(second, width, 1))
    imag = jnp.where(even, pltpu.roll(first, LANES - width, 1), second)
    return real, imag


def gather_cells(ref):
    pieces = [ref[x, g] for g in GROUP_ORDER for x in range(ref.shape[0])]
    return jnp.concatenate(pieces, axis=0)


def store_spectra(spectra, out_ref, width):
    half = spectra.shape[0] // 2
    first, second = pack_parts(spectra[:half], spectra[half:], width)
    groups = out_ref.shape[0]
    block = half // groups
    for d in range(groups):
        out_ref[d, :block] = first[d * block : (d + 1) * block].astype(out_ref.dtype)
        out_ref[d, block:] = second[d * block : (d + 1) * block].astype(out_ref.dtype)


def load_spectra(ref, width):
    groups = ref.shape[0]
    block = ref.shape[1] // 2
    wide = [ref[s].astype(jnp.float32) for s in range(groups)]
    first = jnp.concatenate([w[:block] for w in wide], axis=0)
    second = jnp.concatenate([w[block:] for w in wide], axis=0)
    real, imag = unpack_parts(first, second, width)
    return jnp.concatenate([real, imag], axis=0).astype(jnp.bfloat16)


def store_tiles(spectra, out_ref, width):
    rows = out_ref.shape[1] // (spectra.shape[1] // LANES)
    for c in range(spectra.shape[1] // LANES):
        store_spectra(
            spectra[:, c * LANES : (c + 1) * LANES],
            out_ref.at[:, c * rows : (c + 1) * rows],
            width,
        )


def load_tiles(in_ref, tiles, width):
    rows = in_ref.shape[1] // tiles
    pieces = [load_spectra(in_ref.at[:, c * rows : (c + 1) * rows], width) for c in range(tiles)]
    return jnp.concatenate(pieces, axis=1)


def analyze_kernel(field_ref, table_ref, out_ref, cells_ref, *, width):
    for c in range(field_ref.shape[1] // 4):
        cells_ref[c * LANES : (c + 1) * LANES] = gather_cells(field_ref.at[:, 4 * c : 4 * c + 4])
    store_tiles(dot(table_ref[0], cells_ref[...], 1, 1), out_ref, width)


def rows_kernel(in_ref, table_ref, out_ref):
    lanes = out_ref.shape[2] // 2
    rows = in_ref.shape[1]
    result = turn(joined(in_ref), table_ref, 0).astype(out_ref.dtype)
    for c in range(2):
        for g in range(out_ref.shape[0]):
            out_ref[g, :, c * lanes : (c + 1) * lanes] = result[
                c * rows : (c + 1) * rows, g * lanes : (g + 1) * lanes
            ]


def rows_back_kernel(in_ref, table_ref, out_ref):
    lanes = out_ref.shape[2] // 2
    rows = in_ref.shape[1]
    result = turn(joined(in_ref), table_ref, 1)
    for d in range(out_ref.shape[0]):
        pair = [
            result[c * rows : (c + 1) * rows, d * lanes : (d + 1) * lanes] for c in range(2)
        ]
        out_ref[d] = jnp.concatenate(pair, axis=1).astype(out_ref.dtype)


def columns_forward(in_ref, table_ref):
    rows = in_ref.shape[1]
    result = turn(joined(in_ref), table_ref, 0)
    for c in range(2):
        yield c, result[c * rows : (c + 1) * rows]


def columns_back(mixed_ref, table_ref, out_ref):
    lanes = out_ref.shape[2] // 2
    rows = mixed_ref.shape[1]
    mixed = jnp.concatenate([mixed_ref[0], mixed_ref[1]], axis=0)
    result = turn(mixed, table_ref, 1).astype(out_ref.dtype)
    for c in range(2):
        for g in range(out_ref.shape[0]):
            out_ref[g, :, c * lanes : (c + 1) * lanes] = result[
                c * rows : (c + 1) * rows, g * lanes : (g + 1) * lanes
            ]


def mix_back_kernel(
    in_ref, table_ref, weight_ref, scale_ref, other_ref, out_ref, spec_ref, grad_ref,
    mixed_ref, f_ref, h_ref,
):
    mix_kernel(
        in_ref, table_ref, weight_ref, scale_ref, out_ref, spec_ref, mixed_ref, backward=True,
        extra=lambda: grads_body(other_ref, spec_ref, grad_ref, f_ref, h_ref, 0),
    )


def mix_kernel(
    in_ref, table_ref, weight_ref, scale_ref, out_ref, spec_ref, mixed_ref, *, backward,
    extra=None,
):
    step = pl.program_id(0)
    block = scale_ref.shape[0]
    channels = weight_ref.shape[1] if backward else weight_ref.shape[0]
    inner = weight_ref.shape[0] if backward else weight_ref.shape[1]
    spans = spec_ref.shape[1] // 2

    @pl.when(step == 0)
    def _():
        for c, result in columns_forward(in_ref, table_ref):
            for t in range(2 * spans):
                piece = result[:, t * LANES : (t + 1) * LANES]
                if backward:
                    for r in range(channels // 2):
                        rows = slice(r * block, (r + 1) * block)
                        spec_ref[c, t, rows] = piece[rows] * scale_ref[...]
                else:
                    spec_ref[c, t] = piece

    if extra is not None:
        extra()

    for t in range(spans):
        lanes = slice(t * LANES, (t + 1) * LANES)
        real = [jnp.zeros((block, LANES), jnp.float32)] * inner
        imag = [jnp.zeros((block, LANES), jnp.float32)] * inner
        for k in range(channels):
            rows = slice(k // 2 * block, (k // 2 + 1) * block)
            spec_real = spec_ref[k % 2, t, rows]
            spec_imag = spec_ref[k % 2, spans + t, rows]
            for n in range(inner):
                w = weight_ref.at[n, k] if backward else weight_ref.at[k, n]
                w_real = w[0, :, lanes].astype(jnp.float32)
                w_imag = w[1, :, lanes].astype(jnp.float32)
                if backward:
                    real[n] = real[n] + (spec_real * w_real + spec_imag * w_imag)
                    imag[n] = imag[n] + (spec_imag * w_real - spec_real * w_imag)
                else:
                    real[n] = real[n] + (spec_real * w_real - spec_imag * w_imag)
                    imag[n] = imag[n] + (spec_real * w_imag + spec_imag * w_real)
        for n in range(inner):
            if not backward:
                real[n] = real[n] * scale_ref[...]
                imag[n] = imag[n] * scale_ref[...]
            rows = pl.ds(pl.multiple_of((step * inner + n) // 2 * block, 8), block)
            mixed_ref[n % 2, rows, lanes] = real[n]
            mixed_ref[n % 2, rows, slice((spans + t) * LANES, (spans + t + 1) * LANES)] = imag[n]

    @pl.when(step == pl.num_programs(0) - 1)
    def _():
        columns_back(mixed_ref, table_ref, out_ref)


def synthesize(in_ref, table_ref, tiles, width):
    spectra = load_tiles(in_ref, tiles, width)
    return dot(spectra, table_ref[0], 0, 0) + dot(spectra, table_ref[1], 0, 0)


def slope_kernel(
    in_ref, cells_ref, cot_ref, point_ref, table_ref, out_ref, hidden_ref, preact_ref, *, width
):
    tiles = cells_ref.shape[0] // LANES
    preact_ref[...] = synthesize(in_ref, table_ref, tiles, width) + dot(
        point_ref[...], cells_ref[...]
    )

    def step(c, carry):
        rows = pl.ds(pl.multiple_of(c * LANES, LANES), LANES)
        slope = gelu_slope(preact_ref[rows])
        pieces = [cot_ref[x, 4 * c + g] for g in GROUP_ORDER for x in range(cot_ref.shape[0])]
        cot = jnp.concatenate(pieces, axis=0).astype(jnp.float32)
        hidden_ref[rows] = (cot * slope).astype(jnp.bfloat16)
        return carry

    lax.fori_loop(0, tiles, step, 0)
    store_tiles(dot(table_ref[0], hidden_ref[...], 1, 1), out_ref, width)


def final_kernel(in_ref, hidden_ref, point_ref, table_ref, out_ref, *, width):
    tiles = hidden_ref.shape[0] // LANES
    total = synthesize(in_ref, table_ref, tiles, width)
    total = total + dot(point_ref[...], hidden_ref[...], 0, 0)
    x_local, channels, y_local, _ = out_ref.shape
    total = total.astype(out_ref.dtype)
    for n in range(channels):
        channel = n // 4 * 4 + GROUP_ORDER[n % 4]
        for x in range(x_local):
            start = (n * x_local + x) * y_local
            out_ref[x, channel] = total[start : start + y_local]


def point_kernel(weight_ref, out_ref, *, width):
    rows, channels = out_ref.shape[0], weight_ref.shape[0]
    cell = lax.broadcasted_iota(jnp.int32, (rows, channels), 0) // width
    slot = cell % 4
    channel = cell // 4 * 4 + slot // 2 + slot % 2 * 2
    pick = (channel == lax.broadcasted_iota(jnp.int32, (rows, channels), 1)).astype(jnp.bfloat16)
    left = dot(pick, weight_ref[...], 1, 1).astype(jnp.bfloat16)
    full = dot(left, pick, 1, 1)
    row = lax.broadcasted_iota(jnp.int32, (rows, rows), 0) % width
    column = lax.broadcasted_iota(jnp.int32, (rows, rows), 1) % width
    out_ref[...] = jnp.where(row == column, full, 0.0).astype(jnp.bfloat16)


def pack_body(in_ref, out_ref):
    for i in range(in_ref.shape[1]):
        for p in range(2):
            out_ref[i, :, p] = pltpu.einshape("omky->om(ky)", in_ref[p, i])


def pack_first_kernel(in_ref, out_ref):
    pack_body(in_ref, out_ref)


def pack_rest_kernel(in_ref, _, out_ref):
    pack_body(in_ref, out_ref)


def spread_modes(spec_ref, tile_ref, m):
    count = tile_ref.shape[2] // 8
    block = spec_ref.shape[2] // count
    for c in range(2):
        for p in range(2):
            for k in range(8):
                start = (p * 8 + k) * KY
                piece = spec_ref[c, start // LANES, pl.ds(m, count, stride=block), :]
                start = start % LANES
                tile_ref[c, p, pl.ds(k, count, stride=8), :KY] = piece[:, start : start + KY]


def grads_body(f_spec_ref, h_spec_ref, out_ref, f_ref, h_ref, first):
    channels = out_ref.shape[1]
    mode = pl.program_id(0) + first
    spread_modes(f_spec_ref, f_ref, mode)
    spread_modes(h_spec_ref, h_ref, mode)

    def step(i, carry):
        rows = pl.ds(pl.multiple_of(i // 2 * 8, 8), 8)
        f_real = f_ref[i % 2, 0, rows, :KY]
        f_imag = f_ref[i % 2, 1, rows, :KY]
        for o in range(channels):
            h_real = h_ref[o % 2, 0, o // 2 * 8 : o // 2 * 8 + 8, :KY]
            h_imag = h_ref[o % 2, 1, o // 2 * 8 : o // 2 * 8 + 8, :KY]
            out_ref[0, i, o, 0] = f_real * h_real + f_imag * h_imag
            out_ref[1, i, o, 0] = f_real * h_imag - f_imag * h_real
        return carry

    lax.fori_loop(0, channels, step, 0)


def grads_rest_kernel(f_spec_ref, h_spec_ref, _, out_ref, f_ref, h_ref, *, first):
    grads_body(f_spec_ref, h_spec_ref, out_ref, f_ref, h_ref, first)


def routed_kernel(me_ref, *refs, kernel, receive, send, counts, gated):
    refs = list(refs)
    taken = receive[1] if receive else 1
    sources, refs = refs[:taken], refs[taken:]
    more_in, refs = refs[: counts[0]], refs[counts[0] :]
    taken = send[1] if send else 1
    targets, refs = refs[:taken], refs[taken:]
    more_out, refs = refs[: counts[1]], refs[counts[1] :]
    in_ref, out_ref = sources[0], targets[0]
    if send:
        out_ref = refs.pop()
    if receive:
        in_ref = refs.pop()

    def collect():
        for k, source in enumerate(sources):
            axis, groups = receive
            in_ref[lax.rem(me_ref[axis] + (groups - k), groups)] = source[...]

    def spread():
        for k, target in enumerate(targets):
            axis, groups = send
            target[...] = out_ref[lax.rem(me_ref[axis] + k, groups)]

    if receive:
        pl.when(pl.program_id(0) == 0)(collect) if gated else collect()
    kernel(in_ref, *more_in, out_ref, *more_out, *refs)
    if send:
        last = pl.num_programs(0) - 1
        pl.when(pl.program_id(0) == last)(spread) if gated else spread()


def whole(shape):
    return pl.BlockSpec(shape, lambda *_: (0,) * len(shape))


def fits(field, weight, groups_x, groups_y):
    x_local, y_local, channels, cells = field.shape
    block, kx_local = weight.shape[3:5]
    return (
        cells == NZ * NT
        and x_local * y_local * 4 == LANES
        and channels % 4 == 0
        and block % KT == 0
        and block > channels
        and kx_local == 8
        and y_local == 8
        and weight.shape[5] * 4 == LANES
        and block * groups_x == KZ * KT
    )


def fused_device(field, cotangent, weight, point_weight):
    x_local, y_local, channels, cells = field.shape
    groups_x = lax.axis_size("gx")
    groups_y = lax.axis_size("gy")
    block, kx_local, ky = weight.shape[3:]
    cell_total = groups_x * x_local * groups_y * y_local * cells
    width = x_local * y_local
    rows = channels // 2 * block
    lanes = 2 * kx_local * y_local
    plane = kx_local * ky
    bf16, f32 = jnp.bfloat16, jnp.float32
    shape = jax.ShapeDtypeStruct
    params = partial(pltpu.CompilerParams, vmem_limit_bytes=58 * 1024 * 1024)

    table = jnp.asarray(cell_table())
    row_mat = jnp.asarray(row_table(groups_x, x_local, y_local, groups_y))
    column_mat = jnp.asarray(column_table(groups_y, y_local, kx_local))
    scale = jnp.asarray(scale_table(block, LANES, cell_total))

    spec_shape = shape((groups_x, rows, LANES), bf16)
    flat_shape = shape((channels * width, cells), bf16)
    full_shape = shape((2, 2 * plane // LANES, rows, LANES), f32)
    mid_shape = shape((groups_y, rows, 2 * lanes), bf16)

    me = jnp.stack([lax.axis_index("gx"), lax.axis_index("gy")]).astype(jnp.int32)
    axes = {"gx": (0, groups_x), "gy": (1, groups_y)}

    def route(
        kernel, values, more, in_block, out_block, out_shape, more_specs, more_outs,
        receive=None, send=None, grid=(1,), scratch=(), gated=False,
    ):
        def single(spec):
            index = spec.index_map
            return pl.BlockSpec(spec.block_shape[1:], lambda *at: index(*at)[1:])

        scratch = list(scratch)
        in_specs, out_specs, out_shapes = [in_block], [out_block], [out_shape]
        if receive:
            in_specs = [single(in_block)] * axes[receive][1]
            scratch.append(pltpu.VMEM(in_block.block_shape, bf16))
        if send:
            groups = axes[send][1]
            out_specs = [single(out_block)] * groups
            out_shapes = [shape(out_shape.shape[1:], out_shape.dtype)] * groups
            scratch.append(pltpu.VMEM(out_block.block_shape, bf16))
        body = partial(
            routed_kernel,
            kernel=kernel,
            receive=receive and axes[receive],
            send=send and axes[send],
            counts=(len(more), len(more_outs)),
            gated=gated,
        )
        results = pl.pallas_call(
            body,
            grid=grid,
            in_specs=[pl.BlockSpec(memory_space=pltpu.SMEM)] + in_specs + list(more_specs),
            out_specs=out_specs + [spec for spec, _ in more_outs],
            out_shape=out_shapes + [item for _, item in more_outs],
            scratch_shapes=scratch,
            compiler_params=params(),
        )(me, *(values if receive else [values]), *more)
        if send:
            return [list(results[:groups])] + list(results[groups:])
        return list(results)

    def ring(blocks, axis):
        groups = axes[axis][1]
        received = list(blocks)
        for k in sorted(range(1, groups), key=lambda k: -min(k, groups - k)):
            pairs = [(s, (s + k) % groups) for s in range(groups)]
            received[k] = lax.ppermute(blocks[k], axis, pairs)
        return received

    field_rows = field.transpose(0, 2, 1, 3)
    cot_rows = cotangent.transpose(0, 2, 1, 3)

    spectra, flat_field = pl.pallas_call(
        partial(analyze_kernel, width=width),
        out_shape=[spec_shape, flat_shape],
        compiler_params=params(),
        name="analyze",
    )(field_rows, table)

    pack_shape = shape((channels, channels, 2, block, plane), bf16)
    pack_steps = channels // 2
    pack_head = pack_steps * 3 // 5

    def pack_specs(offset):
        return (
            pl.BlockSpec(
                (2, 2, channels, block, kx_local, ky), lambda i: (0, i + offset, 0, 0, 0, 0)
            ),
            pl.BlockSpec((2, channels, 2, block, plane), lambda i: (i + offset, 0, 0, 0, 0)),
        )

    source, target = pack_specs(0)
    packed = pl.pallas_call(
        pack_first_kernel,
        grid=(pack_head,),
        in_specs=[source],
        out_specs=target,
        out_shape=pack_shape,
        compiler_params=params(),
        name="pack_first",
    )(weight)
    source, target = pack_specs(pack_head)
    packed = pl.pallas_call(
        pack_rest_kernel,
        grid=(pack_steps - pack_head,),
        in_specs=[source, pl.BlockSpec(memory_space=pl.ANY)],
        out_specs=target,
        out_shape=pack_shape,
        input_output_aliases={1: 0},
        compiler_params=params(),
        name="pack_rest",
    )(weight, packed)

    point = pl.pallas_call(
        partial(point_kernel, width=width),
        out_shape=shape((channels * width, channels * width), bf16),
        compiler_params=params(),
        name="point",
    )(point_weight)

    def over_x(values):
        return lax.all_to_all(values, "gx", 0, 0, tiled=True)

    def over_y(values):
        return lax.all_to_all(values, "gy", 0, 0, tiled=True)

    spec_full, mid_full = whole(spec_shape.shape), whole(mid_shape.shape)

    def to_rows(values, receive, send):
        kept = shape(mid_shape.shape, bf16 if send else f32)
        return route(
            rows_kernel, values, [row_mat], spec_full, mid_full, kept,
            [whole(row_mat.shape)], [], receive, send,
        )[0]

    def from_rows(values, receive, send):
        return route(
            rows_back_kernel, values, [row_mat], mid_full, spec_full, spec_shape,
            [whole(row_mat.shape)], [], receive, send,
        )[0]

    grad_tile = (2, channels, channels, 1, kx_local, ky)
    grad_shape = shape((2, channels, channels, block, kx_local, ky), f32)
    tiles_scratch = [pltpu.VMEM((2, 2, channels // 2 * kx_local, LANES), f32)] * 2
    mix_scratch = pltpu.VMEM((2, rows, 2 * plane), f32)
    spec_whole = whole(full_shape.shape)

    def at(offset):
        return lambda m: (0, 0, 0, m + offset, 0, 0)

    def mix(values, send):
        w_block = pl.BlockSpec((channels, 2, 2, block, plane), lambda j: (0, j, 0, 0, 0))
        return route(
            partial(mix_kernel, backward=False), values, [column_mat, packed, scale],
            mid_full, mid_full, mid_shape,
            [whole(column_mat.shape), w_block, whole(scale.shape)],
            [(spec_whole, full_shape)], None, send, grid=(channels // 2,),
            scratch=[mix_scratch], gated=True,
        )

    def mix_back(values, spec, receive):
        w_block = pl.BlockSpec((2, channels, 2, block, plane), lambda j: (j, 0, 0, 0, 0))
        return route(
            mix_back_kernel, values, [column_mat, packed, scale, spec],
            mid_full, mid_full, mid_shape,
            [whole(column_mat.shape), w_block, whole(scale.shape), spec_whole],
            [(spec_whole, full_shape), (pl.BlockSpec(grad_tile, at(0)), grad_shape)],
            receive, None, grid=(channels // 2,),
            scratch=[mix_scratch, *tiles_scratch], gated=True,
        )

    def grads(spec, other, held, first, count):
        return pl.pallas_call(
            partial(grads_rest_kernel, first=first),
            grid=(count,),
            in_specs=[spec_whole, spec_whole, pl.BlockSpec(memory_space=pl.ANY)],
            out_specs=pl.BlockSpec(grad_tile, at(first)),
            out_shape=grad_shape,
            input_output_aliases={2: 0},
            scratch_shapes=tiles_scratch,
            compiler_params=params(),
        )(spec, other, held)

    values = over_y(to_rows(over_x(spectra), None, None))
    mixed, forward_spec = mix(values, "gy")
    back = from_rows(ring(mixed, "gy"), "gy", "gx")
    hidden_spectra, hidden = route(
        partial(slope_kernel, width=width), ring(back, "gx"),
        [flat_field, cot_rows, point, table], spec_full, spec_full, spec_shape,
        [whole(v.shape) for v in (flat_field, cot_rows, point, table)],
        [(whole(flat_shape.shape), flat_shape)], "gx", "gx",
        scratch=[pltpu.VMEM(flat_shape.shape, f32)],
    )
    values = to_rows(ring(hidden_spectra, "gx"), "gx", "gy")
    mixed, hidden_spec, grad = mix_back(ring(values, "gy"), forward_spec, "gy")
    first = channels // 2
    middle = first + (block - first) * 5 // 14
    grad = grads(forward_spec, hidden_spec, grad, first, middle - first)
    back = from_rows(over_y(mixed), None, None)
    grad_spectral = grads(forward_spec, hidden_spec, grad, middle, block - middle)
    back = over_x(back)
    grad_field = pl.pallas_call(
        partial(final_kernel, width=width),
        out_shape=shape((x_local, channels, y_local, cells), bf16),
        compiler_params=params(),
        name="final",
    )(back, hidden, point, table)
    return grad_field.transpose(0, 2, 1, 3), grad_spectral


def per_device(field, cotangent, spectral_weight, point_weight):
    groups = lax.axis_size("gx"), lax.axis_size("gy")
    if fits(field, spectral_weight, *groups):
        return fused_device(field, cotangent, spectral_weight, point_weight)
    return plain_device(field, cotangent, spectral_weight, point_weight)


def solution(mesh):
    placed = (
        P("gx", "gy", None, None),
        P("gx", "gy", None, None),
        P(None, None, None, "gx", "gy", None),
        P(),
    )
    return jax.shard_map(
        per_device,
        mesh=mesh,
        in_specs=placed,
        out_specs=(P("gx", "gy", None, None), P(None, None, None, "gx", "gy", None)),
        check_vma=False,
    )
```

```python
from functools import partial
import math

import jax
import jax.numpy as jnp
import ml_dtypes
import numpy as np
from jax import lax
from jax.experimental import pallas as pl
from jax.experimental.pallas import tpu as pltpu
from jax.sharding import PartitionSpec as P


NZ = 32
NT = 24
KX = 32
KY = 32
KZ = 24
KT = 8


inv_root_two = 1.0 / math.sqrt(2.0)
inv_root_tau = 1.0 / math.sqrt(2.0 * math.pi)


def kept_freq(length, retained):
    series = jnp.arange(retained)
    return jnp.where(series < retained // 2, series, series - retained + length)


def line_angles(length, retained):
    cell_index = jnp.arange(length)
    phases = kept_freq(length, retained)[:, None] * cell_index[None, :] % length
    return phases.astype(jnp.float32) * (2.0 * math.pi / length)


def block_angles():
    cell_total = NZ * NT
    series = jnp.arange(cell_total)
    depth_index = series // NT
    moment = series % NT
    mode_list = jnp.arange(KZ * KT)
    depth_freq = kept_freq(NZ, KZ)[mode_list // KT]
    time_freq = mode_list % KT
    phases = (
        depth_freq[None, :] * depth_index[:, None] % NZ * NT
        + time_freq[None, :] * moment[:, None] % NT * NZ
    )
    return (phases % cell_total).astype(jnp.float32) * (2.0 * math.pi / cell_total)


def mode_scale(mode_list, cell_total):
    return jnp.where(mode_list % KT == 0, 1.0, 2.0).astype(jnp.float32) / cell_total


def twiddle(pattern, cosine, sine, sign, values):
    product = partial(jnp.einsum, pattern, precision=lax.Precision.HIGHEST)
    real_part = values[0]
    imaginary = values[1]
    return jnp.stack(
        [
            product(cosine, real_part) - sign * product(sine, imaginary),
            product(cosine, imaginary) + sign * product(sine, real_part),
        ],
        axis=0,
    )


def channel_mix(spectra, weights):
    widened = weights.astype(jnp.float32)
    product = partial(jnp.einsum, "mkli,iomkl->mklo", precision=lax.Precision.HIGHEST)
    return jnp.stack(
        [
            product(spectra[0], widened[0]) - product(spectra[1], widened[1]),
            product(spectra[0], widened[1]) + product(spectra[1], widened[0]),
        ],
        axis=0,
    )


def weight_grads(forward_spec, hidden_spec):
    product = partial(jnp.einsum, "mkli,mklo->iomkl", precision=lax.Precision.HIGHEST)
    return jnp.stack(
        [
            product(forward_spec[0], hidden_spec[0]) + product(forward_spec[1], hidden_spec[1]),
            product(forward_spec[0], hidden_spec[1]) - product(forward_spec[1], hidden_spec[0]),
        ],
        axis=0,
    )


def back_spectra(hidden_spec, weights):
    widened = weights.astype(jnp.float32)
    product = partial(jnp.einsum, "mklo,iomkl->mkli", precision=lax.Precision.HIGHEST)
    return jnp.stack(
        [
            product(hidden_spec[0], widened[0]) + product(hidden_spec[1], widened[1]),
            product(hidden_spec[1], widened[0]) - product(hidden_spec[0], widened[1]),
        ],
        axis=0,
    )


def gelu_slope(preact):
    return (
        0.5 * (1.0 + jax.scipy.special.erf(preact * inv_root_two))
        + preact * jnp.exp(-0.5 * preact * preact) * inv_root_tau
    )


def plain_device(field, cotangent, spectral_weight, point_weight):
    x_local = field.shape[0]
    y_local = field.shape[1]
    channels = field.shape[2]
    groups_x = lax.axis_size("gx")
    groups_y = lax.axis_size("gy")
    rows_x = x_local * groups_x
    rows_y = y_local * groups_y
    mode_total = KZ * KT
    cell_total = rows_x * rows_y * NZ * NT
    angles = block_angles()
    forward_table = jnp.concatenate([jnp.cos(angles), -jnp.sin(angles)], axis=1).astype(
        jnp.bfloat16
    )
    unscaled = jnp.concatenate([jnp.cos(angles).T, -jnp.sin(angles).T], axis=0)
    mode_list = jnp.arange(mode_total)
    factors = mode_scale(mode_list, cell_total)
    scaled = unscaled * jnp.concatenate([factors, factors])[:, None]
    row_angles = line_angles(rows_x, KX)
    column_angles = line_angles(rows_y, KY)
    row_cos = jnp.cos(row_angles)
    row_sin = jnp.sin(row_angles)
    column_cos = jnp.cos(column_angles)
    column_sin = jnp.sin(column_angles)

    def analyze(cells):
        flat_cells = cells.reshape(-1, cells.shape[3])
        return jnp.einsum(
            "rz,zk->kr", flat_cells, forward_table, preferred_element_type=jnp.float32
        )

    def synthesize(spectra, table):
        flattened = spectra.reshape(2 * mode_total, -1)
        cells = jnp.einsum("kr,kz->rz", flattened, table, precision=lax.Precision.HIGHEST)
        return cells.reshape(x_local, y_local, channels, -1)

    block = mode_total // groups_x

    def forward(cells):
        spectra = analyze(cells).reshape(2, groups_x, block, x_local, y_local * channels)
        spectra = lax.all_to_all(spectra, "gx", split_axis=1, concat_axis=3, tiled=True)
        spectra = spectra.reshape(2, block, rows_x, y_local * channels)
        spectra = twiddle("ka,mar->mkr", row_cos, row_sin, -1.0, spectra)
        spectra = spectra.reshape(2, block, KX, y_local, channels)
        spectra = lax.all_to_all(spectra, "gy", split_axis=2, concat_axis=3, tiled=True)
        return twiddle("lb,mkbc->mklc", column_cos, column_sin, -1.0, spectra)

    def inverse(spectra, table):
        spectra = twiddle("lb,mklc->mkbc", column_cos, column_sin, 1.0, spectra)
        spectra = lax.all_to_all(spectra, "gy", split_axis=3, concat_axis=2, tiled=True)
        spectra = spectra.reshape(2, block, KX, y_local * channels)
        spectra = twiddle("ka,mkr->mar", row_cos, row_sin, 1.0, spectra)
        spectra = lax.all_to_all(spectra, "gx", split_axis=2, concat_axis=1, tiled=True)
        return synthesize(spectra, table)

    forward_spec = forward(field)
    mixed = channel_mix(forward_spec, spectral_weight)
    response = inverse(mixed, scaled)
    preact = response + jnp.einsum(
        "xyiz,io->xyoz", field, point_weight, preferred_element_type=jnp.float32
    )
    hidden = (cotangent.astype(jnp.float32) * gelu_slope(preact)).astype(jnp.bfloat16)
    local_count = forward_spec.shape[1]
    local_modes = lax.axis_index("gx") * local_count + jnp.arange(local_count)
    hidden_spec = forward(hidden) * mode_scale(local_modes, cell_total)[:, None, None, None]
    grad_spectral = weight_grads(forward_spec, hidden_spec)
    backward = inverse(back_spectra(hidden_spec, spectral_weight), unscaled)
    local_part = jnp.einsum(
        "xyoz,io->xyiz", hidden, point_weight, preferred_element_type=jnp.float32
    )
    grad_field = (backward + local_part).astype(jnp.bfloat16)
    return (grad_field, grad_spectral)


LANES = 128
GROUP_ORDER = (0, 2, 1, 3)


def kept_freq_np(length, retained):
    series = np.arange(retained)
    return np.where(series < retained // 2, series, series - retained + length)


TURN_SCALE = 1.62445


def scaled_table(table):
    return (table * TURN_SCALE).astype(ml_dtypes.bfloat16)


def split_table(table):
    high = table.astype(ml_dtypes.bfloat16)
    low = (table - high.astype(np.float64)).astype(ml_dtypes.bfloat16)
    return np.stack([high, low])


def cell_table():
    cells = np.arange(NZ * NT)
    modes = np.arange(KZ * KT)
    depth = kept_freq_np(NZ, KZ)[modes // KT][:, None] * (cells // NT)[None, :] % NZ * NT
    moment = (modes % KT)[:, None] * (cells % NT)[None, :] % NT * NZ
    angles = 2.0 * np.pi * ((depth + moment) % (NZ * NT)) / (NZ * NT)
    return split_table(np.concatenate([np.cos(angles), -np.sin(angles)], axis=0))


def rotation(length, retained):
    phases = np.arange(length)[:, None] * kept_freq_np(length, retained)[None, :] % length
    angles = 2.0 * np.pi * phases / length
    cosine, sine = np.cos(angles), np.sin(angles)
    return np.stack([np.stack([cosine, -sine], axis=1), np.stack([sine, cosine], axis=1)], axis=0)


def row_table(groups_x, x_local, y_local, groups_y):
    turn = rotation(groups_x * x_local, KX)
    turn = turn.reshape(2, groups_x, x_local, 2, groups_y, KX // groups_y)
    full = np.einsum("psxqgk,yz->spxygqkz", turn, np.eye(y_local))
    return scaled_table(full.reshape(groups_x * 2 * x_local * y_local, -1))


def column_table(groups_y, y_local, kx_local):
    turn = rotation(groups_y * y_local, KY).reshape(2, groups_y, y_local, 2, KY)
    full = np.einsum("psyql,kh->spkyqhl", turn, np.eye(kx_local))
    return scaled_table(full.reshape(groups_y * 2 * kx_local * y_local, -1))


def scale_table(block, width, cell_total):
    factors = np.where(np.arange(block) % KT == 0, 1.0, 2.0) / cell_total
    return np.broadcast_to(factors[:, None], (block, width)).astype(np.float32)


def dot(left, right, left_dim=1, right_dim=0):
    return lax.dot_general(
        left, right, (((left_dim,), (right_dim,)), ((), ())), preferred_element_type=jnp.float32
    )


def turn(left, table_ref, right_dim):
    if left.dtype == jnp.bfloat16:
        return dot(left, table_ref[...], 1, right_dim) * (1.0 / TURN_SCALE)
    high = left.astype(jnp.bfloat16)
    low = (left - high.astype(jnp.float32)).astype(jnp.bfloat16)
    both = dot(jnp.concatenate([high, low], axis=0), table_ref[...], 1, right_dim)
    count = left.shape[0]
    return (both[:count] + both[count:]) * (1.0 / TURN_SCALE)


def joined(in_ref):
    half = in_ref.shape[2] // 2
    return jnp.concatenate(
        [
            jnp.concatenate(
                [in_ref[s, :, c * half : (c + 1) * half] for s in range(in_ref.shape[0])], axis=1
            )
            for c in range(2)
        ],
        axis=0,
    )


def even_lanes(rows, width):
    lane = lax.broadcasted_iota(jnp.int32, (rows, LANES), 1)
    return lane // width % 2 == 0


def pack_parts(real, imag, width):
    even = even_lanes(real.shape[0], width)
    first = jnp.where(even, real, pltpu.roll(imag, width, 1))
    second = jnp.where(even, pltpu.roll(real, LANES - width, 1), imag)
    return first, second


def unpack_parts(first, second, width):
    even = even_lanes(first.shape[0], width)
    real = jnp.where(even, first, pltpu.roll(second, width, 1))
    imag = jnp.where(even, pltpu.roll(first, LANES - width, 1), second)
    return real, imag


def gather_cells(ref):
    pieces = [ref[x, g] for g in GROUP_ORDER for x in range(ref.shape[0])]
    return jnp.concatenate(pieces, axis=0)


def store_spectra(spectra, out_ref, width):
    half = spectra.shape[0] // 2
    first, second = pack_parts(spectra[:half], spectra[half:], width)
    groups = out_ref.shape[0]
    block = half // groups
    for d in range(groups):
        out_ref[d, :block] = first[d * block : (d + 1) * block].astype(out_ref.dtype)
        out_ref[d, block:] = second[d * block : (d + 1) * block].astype(out_ref.dtype)


def load_spectra(ref, width):
    groups = ref.shape[0]
    block = ref.shape[1] // 2
    wide = [ref[s].astype(jnp.float32) for s in range(groups)]
    first = jnp.concatenate([w[:block] for w in wide], axis=0)
    second = jnp.concatenate([w[block:] for w in wide], axis=0)
    real, imag = unpack_parts(first, second, width)
    return jnp.concatenate([real, imag], axis=0).astype(jnp.bfloat16)


def store_tiles(spectra, out_ref, width):
    rows = out_ref.shape[1] // (spectra.shape[1] // LANES)
    for c in range(spectra.shape[1] // LANES):
        store_spectra(
            spectra[:, c * LANES : (c + 1) * LANES],
            out_ref.at[:, c * rows : (c + 1) * rows],
            width,
        )


def load_tiles(in_ref, tiles, width):
    rows = in_ref.shape[1] // tiles
    pieces = [load_spectra(in_ref.at[:, c * rows : (c + 1) * rows], width) for c in range(tiles)]
    return jnp.concatenate(pieces, axis=1)


def analyze_kernel(field_ref, table_ref, out_ref, cells_ref, *, width):
    for c in range(field_ref.shape[1] // 4):
        cells_ref[c * LANES : (c + 1) * LANES] = gather_cells(field_ref.at[:, 4 * c : 4 * c + 4])
    store_tiles(dot(table_ref[0], cells_ref[...], 1, 1), out_ref, width)


def rows_kernel(in_ref, table_ref, out_ref):
    lanes = out_ref.shape[2] // 2
    rows = in_ref.shape[1]
    result = turn(joined(in_ref), table_ref, 0).astype(out_ref.dtype)
    for c in range(2):
        for g in range(out_ref.shape[0]):
            out_ref[g, :, c * lanes : (c + 1) * lanes] = result[
                c * rows : (c + 1) * rows, g * lanes : (g + 1) * lanes
            ]


def rows_back_kernel(in_ref, table_ref, out_ref):
    lanes = out_ref.shape[2] // 2
    rows = in_ref.shape[1]
    result = turn(joined(in_ref), table_ref, 1)
    for d in range(out_ref.shape[0]):
        pair = [
            result[c * rows : (c + 1) * rows, d * lanes : (d + 1) * lanes] for c in range(2)
        ]
        out_ref[d] = jnp.concatenate(pair, axis=1).astype(out_ref.dtype)


def columns_forward(in_ref, table_ref):
    rows = in_ref.shape[1]
    result = turn(joined(in_ref), table_ref, 0)
    for c in range(2):
        yield c, result[c * rows : (c + 1) * rows]


def columns_back(mixed_ref, table_ref, out_ref):
    lanes = out_ref.shape[2] // 2
    rows = mixed_ref.shape[1]
    mixed = jnp.concatenate([mixed_ref[0], mixed_ref[1]], axis=0)
    result = turn(mixed, table_ref, 1).astype(out_ref.dtype)
    for c in range(2):
        for g in range(out_ref.shape[0]):
            out_ref[g, :, c * lanes : (c + 1) * lanes] = result[
                c * rows : (c + 1) * rows, g * lanes : (g + 1) * lanes
            ]


def mix_back_kernel(
    in_ref, table_ref, weight_ref, scale_ref, other_ref, out_ref, spec_ref, grad_ref,
    mixed_ref, f_ref, h_ref,
):
    mix_kernel(
        in_ref, table_ref, weight_ref, scale_ref, out_ref, spec_ref, mixed_ref, backward=True,
        extra=lambda: grads_body(other_ref, spec_ref, grad_ref, f_ref, h_ref, 0),
    )


def mix_kernel(
    in_ref, table_ref, weight_ref, scale_ref, out_ref, spec_ref, mixed_ref, *, backward,
    extra=None,
):
    step = pl.program_id(0)
    block = scale_ref.shape[0]
    channels = weight_ref.shape[1] if backward else weight_ref.shape[0]
    inner = weight_ref.shape[0] if backward else weight_ref.shape[1]
    spans = spec_ref.shape[1] // 2

    @pl.when(step == 0)
    def _():
        for c, result in columns_forward(in_ref, table_ref):
            for t in range(2 * spans):
                piece = result[:, t * LANES : (t + 1) * LANES]
                if backward:
                    for r in range(channels // 2):
                        rows = slice(r * block, (r + 1) * block)
                        spec_ref[c, t, rows] = piece[rows] * scale_ref[...]
                else:
                    spec_ref[c, t] = piece

    if extra is not None:
        extra()

    for t in range(spans):
        lanes = slice(t * LANES, (t + 1) * LANES)
        real = [jnp.zeros((block, LANES), jnp.float32)] * inner
        imag = [jnp.zeros((block, LANES), jnp.float32)] * inner
        for k in range(channels):
            rows = slice(k // 2 * block, (k // 2 + 1) * block)
            spec_real = spec_ref[k % 2, t, rows]
            spec_imag = spec_ref[k % 2, spans + t, rows]
            for n in range(inner):
                w = weight_ref.at[n, k] if backward else weight_ref.at[k, n]
                w_real = w[0, :, lanes].astype(jnp.float32)
                w_imag = w[1, :, lanes].astype(jnp.float32)
                if backward:
                    real[n] = real[n] + (spec_real * w_real + spec_imag * w_imag)
                    imag[n] = imag[n] + (spec_imag * w_real - spec_real * w_imag)
                else:
                    real[n] = real[n] + (spec_real * w_real - spec_imag * w_imag)
                    imag[n] = imag[n] + (spec_real * w_imag + spec_imag * w_real)
        for n in range(inner):
            if not backward:
                real[n] = real[n] * scale_ref[...]
                imag[n] = imag[n] * scale_ref[...]
            rows = pl.ds(pl.multiple_of((step * inner + n) // 2 * block, 8), block)
            mixed_ref[n % 2, rows, lanes] = real[n]
            mixed_ref[n % 2, rows, slice((spans + t) * LANES, (spans + t + 1) * LANES)] = imag[n]

    @pl.when(step == pl.num_programs(0) - 1)
    def _():
        columns_back(mixed_ref, table_ref, out_ref)


def synthesize(in_ref, table_ref, tiles, width):
    spectra = load_tiles(in_ref, tiles, width)
    return dot(spectra, table_ref[0], 0, 0) + dot(spectra, table_ref[1], 0, 0)


def slope_kernel(
    in_ref, cells_ref, cot_ref, point_ref, table_ref, out_ref, hidden_ref, preact_ref, *, width
):
    tiles = cells_ref.shape[0] // LANES
    preact_ref[...] = synthesize(in_ref, table_ref, tiles, width) + dot(
        point_ref[...], cells_ref[...]
    )

    def step(c, carry):
        rows = pl.ds(pl.multiple_of(c * LANES, LANES), LANES)
        slope = gelu_slope(preact_ref[rows])
        pieces = [cot_ref[x, 4 * c + g] for g in GROUP_ORDER for x in range(cot_ref.shape[0])]
        cot = jnp.concatenate(pieces, axis=0).astype(jnp.float32)
        hidden_ref[rows] = (cot * slope).astype(jnp.bfloat16)
        return carry

    lax.fori_loop(0, tiles, step, 0)
    store_tiles(dot(table_ref[0], hidden_ref[...], 1, 1), out_ref, width)


def final_kernel(in_ref, hidden_ref, point_ref, table_ref, out_ref, *, width):
    tiles = hidden_ref.shape[0] // LANES
    total = synthesize(in_ref, table_ref, tiles, width)
    total = total + dot(point_ref[...], hidden_ref[...], 0, 0)
    x_local, channels, y_local, _ = out_ref.shape
    total = total.astype(out_ref.dtype)
    for n in range(channels):
        channel = n // 4 * 4 + GROUP_ORDER[n % 4]
        for x in range(x_local):
            start = (n * x_local + x) * y_local
            out_ref[x, channel] = total[start : start + y_local]


def point_kernel(weight_ref, out_ref, *, width):
    rows, channels = out_ref.shape[0], weight_ref.shape[0]
    cell = lax.broadcasted_iota(jnp.int32, (rows, channels), 0) // width
    slot = cell % 4
    channel = cell // 4 * 4 + slot // 2 + slot % 2 * 2
    pick = (channel == lax.broadcasted_iota(jnp.int32, (rows, channels), 1)).astype(jnp.bfloat16)
    left = dot(pick, weight_ref[...], 1, 1).astype(jnp.bfloat16)
    full = dot(left, pick, 1, 1)
    row = lax.broadcasted_iota(jnp.int32, (rows, rows), 0) % width
    column = lax.broadcasted_iota(jnp.int32, (rows, rows), 1) % width
    out_ref[...] = jnp.where(row == column, full, 0.0).astype(jnp.bfloat16)


def pack_body(in_ref, out_ref):
    def step(n, carry):
        out_ref[n // 2, :, n % 2] = pltpu.einshape("omky->om(ky)", in_ref[n % 2, n // 2])
        return carry

    lax.fori_loop(0, 2 * in_ref.shape[1], step, 0)


def pack_first_kernel(in_ref, out_ref):
    pack_body(in_ref, out_ref)


def pack_rest_kernel(in_ref, _, out_ref):
    pack_body(in_ref, out_ref)


def spread_modes(spec_ref, tile_ref, m):
    count = tile_ref.shape[2] // 8
    block = spec_ref.shape[2] // count
    for c in range(2):
        for p in range(2):
            for k in range(8):
                start = (p * 8 + k) * KY
                piece = spec_ref[c, start // LANES, pl.ds(m, count, stride=block), :]
                start = start % LANES
                tile_ref[c, p, pl.ds(k, count, stride=8), :KY] = piece[:, start : start + KY]


def grads_body(f_spec_ref, h_spec_ref, out_ref, f_ref, h_ref, first):
    channels = out_ref.shape[1]
    mode = pl.program_id(0) + first
    spread_modes(f_spec_ref, f_ref, mode)
    spread_modes(h_spec_ref, h_ref, mode)

    def step(i, carry):
        rows = pl.ds(pl.multiple_of(i // 2 * 8, 8), 8)
        f_real = f_ref[i % 2, 0, rows, :KY]
        f_imag = f_ref[i % 2, 1, rows, :KY]
        for o in range(channels):
            h_real = h_ref[o % 2, 0, o // 2 * 8 : o // 2 * 8 + 8, :KY]
            h_imag = h_ref[o % 2, 1, o // 2 * 8 : o // 2 * 8 + 8, :KY]
            out_ref[0, i, o, 0] = f_real * h_real + f_imag * h_imag
            out_ref[1, i, o, 0] = f_real * h_imag - f_imag * h_real
        return carry

    lax.fori_loop(0, channels, step, 0)


def grads_rest_kernel(f_spec_ref, h_spec_ref, _, out_ref, f_ref, h_ref, *, first):
    grads_body(f_spec_ref, h_spec_ref, out_ref, f_ref, h_ref, first)


def routed_kernel(me_ref, *refs, kernel, receive, send, counts, gated):
    refs = list(refs)
    taken = receive[1] if receive else 1
    sources, refs = refs[:taken], refs[taken:]
    more_in, refs = refs[: counts[0]], refs[counts[0] :]
    taken = send[1] if send else 1
    targets, refs = refs[:taken], refs[taken:]
    more_out, refs = refs[: counts[1]], refs[counts[1] :]
    in_ref, out_ref = sources[0], targets[0]
    if send:
        out_ref = refs.pop()
    if receive:
        in_ref = refs.pop()

    def collect():
        for k, source in enumerate(sources):
            axis, groups = receive
            in_ref[lax.rem(me_ref[axis] + (groups - k), groups)] = source[...]

    def spread():
        for k, target in enumerate(targets):
            axis, groups = send
            target[...] = out_ref[lax.rem(me_ref[axis] + k, groups)]

    if receive:
        pl.when(pl.program_id(0) == 0)(collect) if gated else collect()
    kernel(in_ref, *more_in, out_ref, *more_out, *refs)
    if send:
        last = pl.num_programs(0) - 1
        pl.when(pl.program_id(0) == last)(spread) if gated else spread()


def whole(shape):
    return pl.BlockSpec(shape, lambda *_: (0,) * len(shape))


def fits(field, weight, groups_x, groups_y):
    x_local, y_local, channels, cells = field.shape
    block, kx_local = weight.shape[3:5]
    return (
        cells == NZ * NT
        and x_local * y_local * 4 == LANES
        and channels % 4 == 0
        and block % KT == 0
        and block > channels
        and kx_local == 8
        and y_local == 8
        and weight.shape[5] * 4 == LANES
        and block * groups_x == KZ * KT
    )


def fused_device(field, cotangent, weight, point_weight):
    x_local, y_local, channels, cells = field.shape
    groups_x = lax.axis_size("gx")
    groups_y = lax.axis_size("gy")
    block, kx_local, ky = weight.shape[3:]
    cell_total = groups_x * x_local * groups_y * y_local * cells
    width = x_local * y_local
    rows = channels // 2 * block
    lanes = 2 * kx_local * y_local
    plane = kx_local * ky
    bf16, f32 = jnp.bfloat16, jnp.float32
    shape = jax.ShapeDtypeStruct
    params = partial(pltpu.CompilerParams, vmem_limit_bytes=28 * 1024 * 1024)

    table = jnp.asarray(cell_table())
    row_mat = jnp.asarray(row_table(groups_x, x_local, y_local, groups_y))
    column_mat = jnp.asarray(column_table(groups_y, y_local, kx_local))
    scale = jnp.asarray(scale_table(block, LANES, cell_total))

    spec_shape = shape((groups_x, rows, LANES), bf16)
    flat_shape = pltpu.HBM((channels * width, cells), bf16)
    full_shape = pltpu.HBM((2, 2 * plane // LANES, rows, LANES), f32)
    mid_shape = shape((groups_y, rows, 2 * lanes), bf16)

    me = jnp.stack([lax.axis_index("gx"), lax.axis_index("gy")]).astype(jnp.int32)
    axes = {"gx": (0, groups_x), "gy": (1, groups_y)}

    def route(
        kernel, values, more, in_block, out_block, out_shape, more_specs, more_outs,
        receive=None, send=None, grid=(1,), scratch=(), gated=False,
    ):
        def single(spec):
            index = spec.index_map
            return pl.BlockSpec(spec.block_shape[1:], lambda *at: index(*at)[1:])

        scratch = list(scratch)
        in_specs, out_specs, out_shapes = [in_block], [out_block], [out_shape]
        if receive:
            in_specs = [single(in_block)] * axes[receive][1]
            scratch.append(pltpu.VMEM(in_block.block_shape, bf16))
        if send:
            groups = axes[send][1]
            out_specs = [single(out_block)] * groups
            out_shapes = [shape(out_shape.shape[1:], out_shape.dtype)] * groups
            scratch.append(pltpu.VMEM(out_block.block_shape, bf16))
        body = partial(
            routed_kernel,
            kernel=kernel,
            receive=receive and axes[receive],
            send=send and axes[send],
            counts=(len(more), len(more_outs)),
            gated=gated,
        )
        results = pl.pallas_call(
            body,
            grid=grid,
            in_specs=[pl.BlockSpec(memory_space=pltpu.SMEM)] + in_specs + list(more_specs),
            out_specs=out_specs + [spec for spec, _ in more_outs],
            out_shape=out_shapes + [item for _, item in more_outs],
            scratch_shapes=scratch,
            compiler_params=params(),
        )(me, *(values if receive else [values]), *more)
        if send:
            return [list(results[:groups])] + list(results[groups:])
        return list(results)

    def ring(blocks, axis):
        groups = axes[axis][1]
        received = list(blocks)
        for k in sorted(range(1, groups), key=lambda k: -min(k, groups - k)):
            pairs = [(s, (s + k) % groups) for s in range(groups)]
            received[k] = lax.ppermute(blocks[k], axis, pairs)
        return received

    def resident(values):
        return pltpu.with_memory_space_constraint(values, pltpu.HBM)

    field_rows = resident(field.transpose(0, 2, 1, 3))
    cot_rows = resident(cotangent.transpose(0, 2, 1, 3))
    table, row_mat, column_mat = resident(table), resident(row_mat), resident(column_mat)

    spectra, flat_field = pl.pallas_call(
        partial(analyze_kernel, width=width),
        out_shape=[spec_shape, flat_shape],
        compiler_params=params(),
        name="analyze",
    )(field_rows, table)

    pack_shape = pltpu.HBM((channels, channels, 2, block, plane), bf16)
    pack_steps = channels // 2
    pack_head = pack_steps * 3 // 5

    def pack_specs(offset):
        return (
            pl.BlockSpec(
                (2, 2, channels, block, kx_local, ky), lambda i: (0, i + offset, 0, 0, 0, 0)
            ),
            pl.BlockSpec((2, channels, 2, block, plane), lambda i: (i + offset, 0, 0, 0, 0)),
        )

    source, target = pack_specs(0)
    packed = pl.pallas_call(
        pack_first_kernel,
        grid=(pack_head,),
        in_specs=[source],
        out_specs=target,
        out_shape=pack_shape,
        compiler_params=params(),
        name="pack_first",
    )(weight)
    source, target = pack_specs(pack_head)
    packed = pl.pallas_call(
        pack_rest_kernel,
        grid=(pack_steps - pack_head,),
        in_specs=[source, pl.BlockSpec(memory_space=pltpu.HBM)],
        out_specs=target,
        out_shape=pack_shape,
        input_output_aliases={1: 0},
        compiler_params=params(),
        name="pack_rest",
    )(weight, packed)
    packed = resident(packed)

    point = pl.pallas_call(
        partial(point_kernel, width=width),
        out_shape=shape((channels * width, channels * width), bf16),
        compiler_params=params(),
        name="point",
    )(point_weight)

    def over_x(values):
        return lax.all_to_all(values, "gx", 0, 0, tiled=True)

    def over_y(values):
        return lax.all_to_all(values, "gy", 0, 0, tiled=True)

    spec_full, mid_full = whole(spec_shape.shape), whole(mid_shape.shape)

    def to_rows(values, receive, send):
        kept = shape(mid_shape.shape, bf16 if send else f32)
        return route(
            rows_kernel, values, [row_mat], spec_full, mid_full, kept,
            [whole(row_mat.shape)], [], receive, send,
        )[0]

    def from_rows(values, receive, send):
        return route(
            rows_back_kernel, values, [row_mat], mid_full, spec_full, spec_shape,
            [whole(row_mat.shape)], [], receive, send,
        )[0]

    grad_tile = (2, channels, channels, 1, kx_local, ky)
    grad_shape = pltpu.HBM((2, channels, channels, block, kx_local, ky), f32)
    tiles_scratch = [pltpu.VMEM((2, 2, channels // 2 * kx_local, LANES), f32)] * 2
    mix_scratch = pltpu.VMEM((2, rows, 2 * plane), f32)
    spec_whole = whole(full_shape.shape)

    def at(offset):
        return lambda m: (0, 0, 0, m + offset, 0, 0)

    def mix(values, send):
        w_block = pl.BlockSpec((channels, 2, 2, block, plane), lambda j: (0, j, 0, 0, 0))
        return route(
            partial(mix_kernel, backward=False), values, [column_mat, packed, scale],
            mid_full, mid_full, mid_shape,
            [whole(column_mat.shape), w_block, whole(scale.shape)],
            [(spec_whole, full_shape)], None, send, grid=(channels // 2,),
            scratch=[mix_scratch], gated=True,
        )

    def mix_back(values, spec, receive):
        w_block = pl.BlockSpec((2, channels, 2, block, plane), lambda j: (j, 0, 0, 0, 0))
        return route(
            mix_back_kernel, values, [column_mat, packed, scale, spec],
            mid_full, mid_full, mid_shape,
            [whole(column_mat.shape), w_block, whole(scale.shape), spec_whole],
            [(spec_whole, full_shape), (pl.BlockSpec(grad_tile, at(0)), grad_shape)],
            receive, None, grid=(channels // 2,),
            scratch=[mix_scratch, *tiles_scratch], gated=True,
        )

    def grads(spec, other, held, first, count):
        return pl.pallas_call(
            partial(grads_rest_kernel, first=first),
            grid=(count,),
            in_specs=[spec_whole, spec_whole, pl.BlockSpec(memory_space=pl.ANY)],
            out_specs=pl.BlockSpec(grad_tile, at(first)),
            out_shape=grad_shape,
            input_output_aliases={2: 0},
            scratch_shapes=tiles_scratch,
            compiler_params=params(),
        )(spec, other, held)

    values = over_y(to_rows(over_x(spectra), None, None))
    mixed, forward_spec = mix(values, "gy")
    back = from_rows(ring(mixed, "gy"), "gy", "gx")
    flat_field = resident(flat_field)
    hidden_spectra, hidden = route(
        partial(slope_kernel, width=width), ring(back, "gx"),
        [flat_field, cot_rows, point, table], spec_full, spec_full, spec_shape,
        [whole(v.shape) for v in (flat_field, cot_rows, point, table)],
        [(whole(flat_shape.shape), flat_shape)], "gx", "gx",
        scratch=[pltpu.VMEM(flat_shape.shape, f32)],
    )
    values = to_rows(ring(hidden_spectra, "gx"), "gx", "gy")
    forward_spec = resident(forward_spec)
    mixed, hidden_spec, grad = mix_back(ring(values, "gy"), forward_spec, "gy")
    hidden, forward_spec, hidden_spec = map(resident, (hidden, forward_spec, hidden_spec))
    first = channels // 2
    middle = first + (block - first) * 5 // 14
    grad = grads(forward_spec, hidden_spec, grad, first, middle - first)
    back = from_rows(over_y(mixed), None, None)
    grad_spectral = grads(forward_spec, hidden_spec, grad, middle, block - middle)
    back = over_x(back)
    grad_field = pl.pallas_call(
        partial(final_kernel, width=width),
        out_shape=shape((x_local, channels, y_local, cells), bf16),
        compiler_params=params(),
        name="final",
    )(back, hidden, point, table)
    return grad_field.transpose(0, 2, 1, 3), grad_spectral


def per_device(field, cotangent, spectral_weight, point_weight):
    groups = lax.axis_size("gx"), lax.axis_size("gy")
    if fits(field, spectral_weight, *groups):
        return fused_device(field, cotangent, spectral_weight, point_weight)
    return plain_device(field, cotangent, spectral_weight, point_weight)


def solution(mesh):
    placed = (
        P("gx", "gy", None, None),
        P("gx", "gy", None, None),
        P(None, None, None, "gx", "gy", None),
        P(),
    )
    return jax.shard_map(
        per_device,
        mesh=mesh,
        in_specs=placed,
        out_specs=(P("gx", "gy", None, None), P(None, None, None, "gx", "gy", None)),
        check_vma=False,
    )
```
